256 devices in a mesh: seq: 32 (over z, y), exp: 8 (over x, core).
Axes of the slice: x: 4, y: 4, z: 8, core: 2. Of those that a mesh axis runs over, the one named last changes fastest.
Arguments:
- resid_rows: bfloat16 [8, 128, 3072], P('exp', 'seq'), may hold values from -6 to 6
- query_rows: bfloat16 [8, 128, 3072], P('exp', 'seq'), may hold values from -6 to 6
- key_rows: bfloat16 [8, 4096, 3072], P('exp', 'seq'), may hold values from -6 to 6
- value_rows: bfloat16 [8, 4096, 3072], P('exp', 'seq'), may hold values from -6 to 6
- log_decay: float32 [8, 48, 4096], P('exp', None, 'seq'), may hold values from -1 to 0
- read_pos: int32 [8, 128], P('exp', 'seq'), may hold values from 0 to 4095, as said below
- expert_ids: int32 [8, 128, 2], P('exp', 'seq'), may hold values from 0 to 7, all different within a row; in each aligned block of 4 rows (0 to 3, 4 to 7, ..., all dimensions but the last counted through in order) at most 2 rows name the same one
- pair_order: int32 [8], replicated, may hold values from 0 to 7, each once
- lengths: int32 [8], replicated, may hold values from 1 to 4096
- norm_gain: bfloat16 [3072], replicated, may hold values from 0.5 to 1.5
- router_weight: bfloat16 [3072, 8], replicated, may hold values from -0.109375 to 0.109375
- score_weight: bfloat16 [3072], replicated, may hold values from -0.109375 to 0.109375
- gate_weight: bfloat16 [8, 3072, 9216], P('exp', None, 'seq'), may hold values from -0.109375 to 0.109375
- up_weight: bfloat16 [8, 3072, 9216], P('exp', None, 'seq'), may hold values from -0.109375 to 0.109375
- down_weight: bfloat16 [8, 9216, 3072], P('exp', 'seq'), may hold values from -0.0625 to 0.0625
Outputs:
- pair_loss: float32 [], replicated
- grad_query: float32 [8, 128, 3072], P('exp', 'seq')
- grad_resid: float32 [8, 128, 3072], P('exp', 'seq')
- grad_keys: bfloat16 [8, 4096, 3072], P('exp', 'seq')
- grad_values: bfloat16 [8, 4096, 3072], P('exp', 'seq')
The draws below stay inside these ranges and needn't reach their ends.
Inputs may be any that keep to these rules, and one draw needn't show every extreme that they name: `read_pos`: each aligned block j of 4 entries of a sequence holds strictly increasing positions from j * 128 to (j + 1) * 128 - 1, the last of them being (j + 1) * 128 - 1. `expert_ids`: the two entries of a row differ; in the rows of one device (aligned blocks of 4 rows) no expert is named by more than 2 rows. `pair_order`: each sequence appears once.
All inputs are finite; a program needn't handle non-finite values.
Results may differ from the reference program's by a relative error of at most 0.018.
Values may be sent and summed in bfloat16 or wider, within the bound.
No kernel may reach another device: no remote copies, remote signals or barrier semaphores. Data moves between devices by JAX's collectives and lax.ppermute only.
A program may use at most 128 MiB of HBM per device.

```python
import math
import jax
import jax.numpy as jnp
import numpy as np
from jax import lax

D = 3072
FOCUS_CHANNELS = 48
HEAD_DIM = 64
FF = 9216
TOK_DEV = 128
READ_DEV = 4
TEXT_SPAN = 4096
READS = 128
TEXT_TOTAL = 8
EXPERTS = 8
CAP = 2
N_SEQ = 32


def draw_log_decay(key, part):
    boundary_indices = jax.random.split(key, 7)
    group_count = TEXT_SPAN // TOK_DEV
    fast_share = 0.5
    picked = jax.random.uniform(boundary_indices[0], (TEXT_TOTAL, FOCUS_CHANNELS, 1))
    fast_rate = jnp.exp(jax.random.uniform(boundary_indices[1], (TEXT_TOTAL, FOCUS_CHANNELS, 1), minval=jnp.log(1.0 / 50.0), maxval=jnp.log(1.0 / 30.0)))
    slow_rate = jnp.exp(jax.random.uniform(boundary_indices[2], (TEXT_TOTAL, FOCUS_CHANNELS, 1), minval=jnp.log(0.05 / TEXT_SPAN), maxval=jnp.log(0.6 / TEXT_SPAN)))
    forgetting_speed = jnp.where(picked < fast_share, fast_rate, slow_rate)
    block_factor = jnp.exp(jax.random.uniform(boundary_indices[3], (TEXT_TOTAL, FOCUS_CHANNELS, group_count), minval=-0.7, maxval=0.7))
    scatter_breadth = jnp.repeat(block_factor, TOK_DEV, axis=2)
    rough_guess = jax.random.uniform(boundary_indices[4], (TEXT_TOTAL, FOCUS_CHANNELS, TEXT_SPAN), minval=0.5, maxval=1.5)
    period_flag = jax.random.uniform(boundary_indices[5], (TEXT_TOTAL, FOCUS_CHANNELS, TEXT_SPAN)) < 2.0 / TEXT_SPAN
    period_span = jnp.log(jax.random.uniform(boundary_indices[6], (TEXT_TOTAL, FOCUS_CHANNELS, TEXT_SPAN), minval=0.5, maxval=0.8))
    return (-forgetting_speed * scatter_breadth * rough_guess + jnp.where(period_flag, period_span, 0.0)).astype(jnp.float32)


def draw_read_pos(key, part):
    group_count = TEXT_SPAN // TOK_DEV
    boundary_indices = jax.random.split(key, TEXT_TOTAL * group_count)

    def choose_rows(sub_key):
        shuffled = jax.random.permutation(sub_key, TOK_DEV - 1)
        return jnp.sort(shuffled[:READ_DEV - 1]).astype(jnp.int32)
    picked = jax.vmap(choose_rows)(boundary_indices).reshape(TEXT_TOTAL, group_count, READ_DEV - 1)
    closing = jnp.full((TEXT_TOTAL, group_count, 1), TOK_DEV - 1, jnp.int32)
    inside = jnp.concatenate([picked, closing], axis=2)
    offset = (jnp.arange(group_count, dtype=jnp.int32) * TOK_DEV)[None, :, None]
    return (inside + offset).reshape(TEXT_TOTAL, READS).astype(jnp.int32)


def touch_ends(values, own_key, least, high):
    longest = values.shape.index(max(values.shape))
    spots = []
    for shift in (0, 1):
        where = [jax.random.randint(jax.random.fold_in(own_key, axis), (), 0, length) for axis, length in enumerate(values.shape)]
        where[longest] = (where[longest] + shift) % values.shape[longest]
        spots.append(tuple(where))
    return values.at[spots[0]].set(least).at[spots[1]].set(high)


def level_of(key, shape, cuts, least, high):
    factor_of, own = 1.0, jax.random.fold_in(key, 6)
    for position, parts in cuts:
        steps = jnp.exp(jax.random.uniform(jax.random.fold_in(own, position), (parts,), jnp.float32, least / len(cuts), high / len(cuts)))
        factor_of = factor_of * jnp.repeat(steps, shape[position] // parts).reshape([-1 if axis == position else 1 for axis in range(len(shape))])
    return factor_of


def assign_block(rng, own, number, rows, number_of, top, bound, slope):
    order = jax.random.permutation(rng, number_of)
    crowded, usual = shares(number_of, rows * top, bound, slope, True), shares(number_of, rows * top, bound, slope, False)
    places = jnp.arange(number_of)

    def named(sizes, turn):
        used = int((sizes > 0).sum())
        fixed = max(1, used // 4)
        passed = fixed + (places - fixed + turn * (used - fixed)) % max(1, number_of - fixed)
        return jnp.zeros((number_of,), jnp.int32).at[order[jnp.where(places < fixed, places, passed)]].set(jnp.asarray(sizes, jnp.int32))

    sizes = jnp.where(number % 4 == 0, named(crowded, number // 4), named(usual, number - number // 4 - 1))
    mixed = jax.random.permutation(jax.random.fold_in(own, 3), number_of)
    source_of, taker = mixed[0:number_of // 2 * 2:2], mixed[1:number_of // 2 * 2:2]
    room = jnp.minimum(sizes[source_of] - 1, bound - sizes[taker]) // 2
    room = jnp.where((source_of == order[0]) | (taker == order[0]) | (sizes[taker] == 0), 0, jnp.maximum(room, 0))
    passed = jax.random.randint(jax.random.fold_in(own, 4), (number_of // 2,), 0, 1 << 20) % (room + 1)
    sizes = sizes.at[source_of].add(-passed).at[taker].add(passed)
    members = jnp.searchsorted(jnp.cumsum(sizes), jnp.arange(rows * top), side="right").astype(jnp.int32)
    table = members.reshape(top, rows).T
    table = table[jax.random.permutation(jax.random.fold_in(own, 1), rows)]
    turn = jax.random.randint(jax.random.fold_in(own, 2), (rows, 1), 0, top)
    return jnp.take_along_axis(table, (jnp.arange(top)[None, :] + turn) % top, axis=1)


def shares(amount, total, limit, slope, full):
    portions = [(1 << 20) // math.isqrt(rank ** slope) + 1 for rank in range(1, amount + 1)]
    largest = limit if full else min(limit, max(-(-total // amount), total * portions[0] // sum(portions)))
    least = 1 if total - largest >= amount - 1 else 0
    holding, rest = [largest] + [least] * (amount - 1), total - largest - least * (amount - 1)
    while rest > 0:
        movable = [i for i in range(1, amount) if holding[i] < largest] or [i for i in range(1, amount) if holding[i] < limit]
        whole, left = sum([portions[i] for i in movable]), rest
        for i in movable:
            more = min(limit - holding[i], max(1, left * portions[i] // whole), rest)
            holding[i] = holding[i] + more
            rest = rest - more
    return np.array(holding)


def normal_values(key, dims, width, bound, shards=(), kind=jnp.bfloat16):
    result = width * jax.random.normal(key, dims, jnp.float32)
    if shards:
        result = result * level_of(key, dims, shards, -0.22, 0.18)
    return jnp.clip(result, -bound, bound).astype(kind)


def setup_inputs(seed: int = 0) -> dict:
    seeds = jax.random.split(jax.random.key(seed), 16)
    resid_rows = normal_values(seeds[0], (TEXT_TOTAL, READS, D), 1.0, 6.0, ((0, 8), (1, 32)))
    query_rows = normal_values(seeds[1], (TEXT_TOTAL, READS, D), 1.0, 6.0, ((0, 8), (1, 32)))
    key_rows = normal_values(seeds[2], (TEXT_TOTAL, TEXT_SPAN, D), 1.0, 6.0, ((0, 8), (1, 32)))
    value_rows = normal_values(seeds[3], (TEXT_TOTAL, TEXT_SPAN, D), 1.0, 6.0, ((0, 8), (1, 32)))
    log_decay = draw_log_decay(jax.random.fold_in(seeds[15], 71), 0)
    read_pos = draw_read_pos(jax.random.fold_in(seeds[15], 71), 0)
    expert_ids_keys = jax.random.split(jax.random.fold_in(seeds[6], 1), TEXT_TOTAL * READS // READ_DEV)
    expert_ids_turns = jax.random.permutation(jax.random.fold_in(seeds[6], 3), TEXT_TOTAL * READS // READ_DEV)
    expert_ids = jax.vmap(lambda own, number: assign_block(jax.random.fold_in(seeds[6], 2), own, number, READ_DEV, EXPERTS, 2, CAP, 1))(expert_ids_keys, expert_ids_turns).reshape((TEXT_TOTAL, READS, 2))
    pair_order = jax.random.permutation(seeds[7], TEXT_TOTAL).astype(jnp.int32)
    lengths = touch_ends(jax.random.randint(seeds[8], (TEXT_TOTAL,), 1, TEXT_SPAN + 1), jax.random.fold_in(seeds[8], 1), 1, TEXT_SPAN).astype(jnp.int32)
    norm_gain = jnp.clip(1.0 + 0.1 * jax.random.normal(seeds[9], (D,), jnp.float32), 0.5, 1.5).astype(jnp.bfloat16)
    router_weight = normal_values(seeds[10], (D, EXPERTS), D ** -0.5, 0.109375)
    score_weight = normal_values(seeds[11], (D,), D ** -0.5, 0.109375)
    gate_weight = normal_values(seeds[12], (EXPERTS, D, FF), D ** -0.5, 0.109375, ((0, 8), (2, 32)))
    up_weight = normal_values(seeds[13], (EXPERTS, D, FF), D ** -0.5, 0.109375, ((0, 8), (2, 32)))
    down_weight = normal_values(seeds[14], (EXPERTS, FF, D), FF ** -0.5, 0.0625, ((0, 8), (1, 32)))
    return dict(resid_rows=resid_rows, query_rows=query_rows, key_rows=key_rows, value_rows=value_rows, log_decay=log_decay, read_pos=read_pos, expert_ids=expert_ids, pair_order=pair_order, lengths=lengths, norm_gain=norm_gain, router_weight=router_weight, score_weight=score_weight, gate_weight=gate_weight, up_weight=up_weight, down_weight=down_weight)


PRECISE = lax.Precision.HIGHEST
EPSILON = 1e-06
LENGTH_WEIGHT = 4.0
SCORE_SCALE = 256.0

def readout_weights(cumulated, places):
    positions = jnp.arange(cumulated.shape[1], dtype=jnp.int32)
    one_hot = (places[:, None] == positions[None, :]).astype(jnp.float32)
    at_read = jnp.dot(cumulated, one_hot.T, precision=PRECISE)
    allowed = positions[None, :] <= places[:, None]
    exponent = jnp.where(allowed[None], at_read[:, :, None] - cumulated[:, None, :], -1e+30)
    return (at_read, jnp.exp(exponent))

def preference_loss(rewards, pair_order, lengths, total_length):
    count = rewards.shape[0]
    ordering = (pair_order[:, None] == jnp.arange(count, dtype=jnp.int32)[None, :]).astype(jnp.float32)
    ranked = jnp.dot(ordering, rewards, precision=PRECISE).reshape(count // 2, 2)
    fitted = jnp.mean(jax.nn.softplus(ranked[:, 1] - ranked[:, 0]))
    share = lengths.astype(jnp.float32) / total_length
    scatter_breadth = jnp.mean((rewards - jnp.mean(rewards)) * (share - jnp.mean(share)))
    return fitted + LENGTH_WEIGHT * scatter_breadth * scatter_breadth

def group_terms(key_group, value_group, decay_group, query_group, place_group, offset):
    cumulated = jnp.cumsum(decay_group, axis=1)
    tail_decay = jnp.exp(cumulated[:, -1:] - cumulated).T[:, :, None]
    own_state = jnp.einsum('thi,thj->hij', key_group * tail_decay, value_group, precision=PRECISE)
    at_read, weight = readout_weights(cumulated, place_group - offset)
    lift = jnp.exp(at_read).T[:, :, None]
    query_key = jnp.einsum('rhi,thi->hrt', query_group.astype(jnp.bfloat16), key_group.astype(jnp.bfloat16), preferred_element_type=jnp.float32) / HEAD_DIM
    return (jnp.exp(cumulated[:, -1]), tail_decay, own_state, lift, weight, query_key)

def split_sequence(query_seq, key_seq, value_seq, decay_seq, place_seq):
    key_groups = key_seq.astype(jnp.float32).reshape(N_SEQ, TOK_DEV, FOCUS_CHANNELS, HEAD_DIM)
    value_groups = value_seq.astype(jnp.float32).reshape(N_SEQ, TOK_DEV, FOCUS_CHANNELS, HEAD_DIM)
    query_groups = query_seq.astype(jnp.float32).reshape(N_SEQ, READ_DEV, FOCUS_CHANNELS, HEAD_DIM)
    decay_groups = decay_seq.reshape(FOCUS_CHANNELS, N_SEQ, TOK_DEV).transpose(1, 0, 2)
    place_groups = place_seq.reshape(N_SEQ, READ_DEV)
    offsets = jnp.arange(N_SEQ, dtype=jnp.int32) * TOK_DEV
    return (key_groups, value_groups, decay_groups, query_groups, place_groups, offsets)

def seq_forward(packed):
    groups = split_sequence(*packed)

    def advance(state, pieces):
        key_group, value_group, decay_group, query_group, place_group, offset = pieces
        decay_total, tail_decay, own_state, lift, weight, query_key = group_terms(key_group, value_group, decay_group, query_group, place_group, offset)
        attended = jnp.einsum('hrt,thj->rhj', weight * query_key, value_group, precision=PRECISE)
        attended = attended + lift * jnp.einsum('rhi,hij->rhj', query_group, state, precision=PRECISE) / HEAD_DIM
        return (decay_total[:, None, None] * state + own_state, (attended, state))
    start = jnp.zeros((FOCUS_CHANNELS, HEAD_DIM, HEAD_DIM), jnp.float32)
    _, (attended, states) = lax.scan(advance, start, groups)
    return (attended.reshape(READS, D), states)

def seq_backward(packed):
    query_seq, key_seq, value_seq, decay_seq, place_seq, grad_seq = packed
    _, states = seq_forward((query_seq, key_seq, value_seq, decay_seq, place_seq))
    groups = split_sequence(query_seq, key_seq, value_seq, decay_seq, place_seq)
    grad_groups = grad_seq.astype(jnp.float32).reshape(N_SEQ, READ_DEV, FOCUS_CHANNELS, HEAD_DIM)

    def retreat(suffix, pieces):
        key_group, value_group, decay_group, query_group, place_group, offset, grad_group, state = pieces
        decay_total, tail_decay, own_state, lift, weight, query_key = group_terms(key_group, value_group, decay_group, query_group, place_group, offset)
        grad_dot = jnp.einsum('rhj,thj->hrt', grad_group.astype(jnp.bfloat16), value_group.astype(jnp.bfloat16), preferred_element_type=jnp.float32) / HEAD_DIM
        grad_query = jnp.einsum('hrt,thi->rhi', weight * grad_dot, key_group, precision=PRECISE)
        grad_query = grad_query + lift * jnp.einsum('rhj,hij->rhi', grad_group, state, precision=PRECISE) / HEAD_DIM
        grad_keys = jnp.einsum('hrt,rhi->thi', weight * grad_dot, query_group, precision=PRECISE)
        grad_keys = grad_keys + tail_decay * jnp.einsum('hij,thj->thi', suffix, value_group, precision=PRECISE)
        grad_values = jnp.einsum('hrt,rhj->thj', weight * query_key, grad_group, precision=PRECISE)
        grad_values = grad_values + tail_decay * jnp.einsum('thi,hij->thj', key_group, suffix, precision=PRECISE)
        summary = jnp.einsum('rhi,rhj->hij', query_group * lift, grad_group, precision=PRECISE) / HEAD_DIM
        return (decay_total[:, None, None] * suffix + summary, (grad_query, grad_keys, grad_values))
    start = jnp.zeros((FOCUS_CHANNELS, HEAD_DIM, HEAD_DIM), jnp.float32)
    _, (grad_query, grad_keys, grad_values) = lax.scan(retreat, start, groups + (grad_groups, states), reverse=True)
    return (grad_query.reshape(READS, D), grad_keys.reshape(TEXT_SPAN, D), grad_values.reshape(TEXT_SPAN, D))

def split_sum(lefts, rights):
    left_parts = tuple((matrix.reshape(matrix.shape[0], N_SEQ, -1).transpose(1, 0, 2) for matrix in lefts))
    right_parts = tuple((matrix.reshape(N_SEQ, -1, matrix.shape[1]) for matrix in rights))
    row_count = lefts[0].shape[0]
    col_count = rights[0].shape[1]

    def accumulate(total, pieces):
        left_piece, right_piece = pieces
        partial_term = jnp.zeros((row_count, col_count), jnp.float32)
        for index in range(len(left_piece)):
            partial_term = partial_term + jnp.dot(left_piece[index], right_piece[index], preferred_element_type=jnp.float32)
        rounded = lax.optimization_barrier(partial_term.astype(jnp.bfloat16))
        return (total + rounded.astype(jnp.float32), None)
    total, _ = lax.scan(accumulate, jnp.zeros((row_count, col_count), jnp.float32), (left_parts, right_parts))
    return total.astype(jnp.bfloat16)

def reference(resid_rows, query_rows, key_rows, value_rows, log_decay, read_pos, expert_ids, pair_order, lengths, norm_gain, router_weight, score_weight, gate_weight, up_weight, down_weight):
    attended = lax.map(lambda packed: seq_forward(packed)[0], (query_rows, key_rows, value_rows, log_decay, read_pos))
    row_count = TEXT_TOTAL * READS
    assign_count = 2 * row_count
    block_count = TEXT_TOTAL * N_SEQ
    residual = (resid_rows.astype(jnp.float32) + attended).reshape(row_count, D)
    inverse = lax.rsqrt(lax.optimization_barrier(jnp.mean(residual * residual, axis=1, keepdims=True)) + EPSILON)
    unit_rows = residual * inverse
    gain_float = norm_gain.astype(jnp.float32)
    normed = (unit_rows * gain_float).astype(jnp.bfloat16)
    logits = jnp.dot(normed, router_weight, preferred_element_type=jnp.float32)
    pair_ids = expert_ids.reshape(row_count, 2).astype(jnp.int32)
    picks = (pair_ids[:, :, None] == jnp.arange(EXPERTS, dtype=jnp.int32)[None, None, :]).astype(jnp.float32)
    chosen = jnp.einsum('rke,re->rk', picks, logits, precision=PRECISE)
    first = jax.nn.sigmoid(chosen[:, 0] - chosen[:, 1])
    gates = jnp.stack([first, 1.0 - first], axis=1)
    flat_ids = pair_ids.reshape(assign_count)
    hits = (flat_ids[:, None] == jnp.arange(EXPERTS, dtype=jnp.int32)[None, :]).astype(jnp.int32)
    per_block = hits.reshape(block_count, 2 * READ_DEV, EXPERTS)
    earlier = (jnp.cumsum(per_block, axis=1) - per_block).reshape(assign_count, EXPERTS)
    slot_index = lax.optimization_barrier(jnp.sum(earlier * hits, axis=1)).astype(jnp.int32)
    blocks = jnp.arange(assign_count, dtype=jnp.int32) // (2 * READ_DEV)
    target = (blocks * CAP + slot_index).astype(jnp.int32)
    table = jnp.full((EXPERTS, block_count * CAP), assign_count, jnp.int32)
    table = table.at[flat_ids, target].set(jnp.arange(assign_count, dtype=jnp.int32))
    padded_rows = jnp.concatenate([normed, jnp.zeros((1, D), jnp.bfloat16)], axis=0)

    def project_in(index_row, gate_w, up_w):
        taken = padded_rows[index_row // 2]
        pre_gate = jnp.dot(taken, gate_w, preferred_element_type=jnp.float32)
        pre_up = jnp.dot(taken, up_w, preferred_element_type=jnp.float32)
        return (pre_gate, pre_up)

    def expert_forward(packed):
        index_row, gate_w, up_w, down_w = packed
        pre_gate, pre_up = project_in(index_row, gate_w, up_w)
        activated = (jax.nn.silu(pre_gate) * pre_up).astype(jnp.bfloat16)
        return split_sum((activated,), (down_w,))
    expert_slots = lax.map(expert_forward, (table, gate_weight, up_weight, down_weight))
    expert_out = expert_slots[flat_ids, target].reshape(row_count, 2, D).astype(jnp.float32)
    mixed = residual + lax.optimization_barrier(jnp.sum(gates[:, :, None] * expert_out, axis=1))
    score_float = score_weight.astype(jnp.float32)
    score = jnp.dot(mixed, score_float, precision=PRECISE)
    rewards = lax.optimization_barrier(jnp.mean(score.reshape(TEXT_TOTAL, READS), axis=1))
    pair_loss, d_reward = jax.value_and_grad(preference_loss)(rewards, pair_order, lengths, TEXT_SPAN)
    d_mixed = jnp.repeat(SCORE_SCALE * d_reward, READS)[:, None] * score_float[None, :]
    d_out = (gates[:, :, None] * d_mixed[:, None, :]).astype(jnp.bfloat16)
    d_gates = jnp.einsum('rd,rkd->rk', d_mixed, expert_out, precision=PRECISE)
    d_logit = (d_gates[:, 0] - d_gates[:, 1]) * first * (1.0 - first)
    padded_grads = jnp.concatenate([d_out.reshape(assign_count, D), jnp.zeros((1, D), jnp.bfloat16)], axis=0)

    def expert_backward(packed):
        index_row, gate_w, up_w, down_w = packed
        pre_gate, pre_up = project_in(index_row, gate_w, up_w)
        grads_in = padded_grads[index_row]
        d_act = jnp.dot(grads_in, down_w.T, preferred_element_type=jnp.float32)
        gate_sigmoid = jax.nn.sigmoid(pre_gate)
        d_pre_gate = (d_act * pre_up * gate_sigmoid * (1.0 + pre_gate * (1.0 - gate_sigmoid))).astype(jnp.bfloat16)
        d_pre_up = (d_act * pre_gate * gate_sigmoid).astype(jnp.bfloat16)
        return split_sum((d_pre_gate, d_pre_up), (gate_w.T, up_w.T))
    d_in_slots = lax.map(expert_backward, (table, gate_weight, up_weight, down_weight))
    d_in = d_in_slots[flat_ids, target].reshape(row_count, 2, D).astype(jnp.float32)
    columns = jnp.einsum('rke,de->rkd', picks, router_weight.astype(jnp.float32), precision=PRECISE)
    d_normed = lax.optimization_barrier(jnp.sum(d_in, axis=1)) + d_logit[:, None] * (columns[:, 0] - columns[:, 1])
    d_unit = d_normed * gain_float
    grad_resid = d_mixed + inverse * (d_unit - unit_rows * lax.optimization_barrier(jnp.mean(d_unit * unit_rows, axis=1, keepdims=True)))
    d_attended = grad_resid.astype(jnp.bfloat16).reshape(TEXT_TOTAL, READS, D)
    grad_query, grad_keys, grad_values = lax.map(seq_backward, (query_rows, key_rows, value_rows, log_decay, read_pos, d_attended))
    return (pair_loss, grad_query, grad_resid.reshape(TEXT_TOTAL, READS, D), grad_keys.astype(jnp.bfloat16), grad_values.astype(jnp.bfloat16))
```

```python
import jax
import jax.numpy as jnp
import numpy as np
from jax import lax
from jax.experimental import pallas as pl
from jax.experimental.pallas import tpu as pltpu
from jax.sharding import PartitionSpec as P

PRECISE = lax.Precision.HIGHEST
EPSILON = 1e-06
LENGTH_WEIGHT = 4.0
SCORE_SCALE = 256.0
YS = 4
LANES = 128


def receive(value, dz, dy):
    zs = lax.axis_size("seq") // YS
    pairs = [
        (((z + dz) % zs) * YS + (y + dy) % YS, z * YS + y) for z in range(zs) for y in range(YS)
    ]
    return lax.ppermute(value, "seq", pairs)


def split_cols(value):
    half = -(-value.shape[-1] // (2 * LANES)) * LANES
    return value[..., :half], value[..., half:]


def ring_gather(own, axis, count):
    def get(value, step):
        return receive(value, step, 0) if axis == "z" else receive(value, 0, step)

    blocks = [None] * count
    blocks[0] = own
    ahead = behind = own
    for lap in range(1, count // 2):
        ahead, behind = get(ahead, 1), get(behind, -1)
        blocks[lap], blocks[count - lap] = ahead, behind
    first, _ = split_cols(ahead)
    _, second = split_cols(behind)
    blocks[count // 2] = jnp.concatenate([get(first, 1), get(second, -1)], axis=-1)
    return blocks


def add_rounded(left, right):
    return (left.astype(jnp.float32) + right.astype(jnp.float32)).astype(jnp.bfloat16)


def ring_reduce(blocks, axis):
    count = len(blocks)

    def get(value, step):
        return receive(value, step, 0) if axis == "z" else receive(value, 0, step)

    first, second = split_cols(blocks[count // 2])
    first, second = get(first, -1), get(second, 1)
    for lap in range(count // 2 - 1, 0, -1):
        up, down = blocks[lap], blocks[count - lap]
        if lap == count // 2 - 1:
            half = first.shape[-1]
            up = jnp.concatenate([add_rounded(up[..., :half], first), up[..., half:]], axis=-1)
            down = jnp.concatenate(
                [down[..., :half], add_rounded(down[..., half:], second)], axis=-1
            )
        else:
            up, down = add_rounded(up, first), add_rounded(down, second)
        first, second = get(up, -1), get(down, 1)
    total = (
        blocks[0].astype(jnp.float32) + first.astype(jnp.float32) + second.astype(jnp.float32)
    )
    return total.astype(jnp.bfloat16)


def cut_of(width):
    return -(-width // (2 * LANES)) * LANES


def gather_slots(rows):
    zs = lax.axis_size("seq") // YS
    cut = cut_of(rows.shape[-1])
    left = jnp.stack(ring_gather(rows[:, :cut], "y", YS))
    left = jnp.stack(ring_gather(left, "z", zs))
    right = jnp.stack(ring_gather(rows[:, cut:], "z", zs))
    right = jnp.stack(ring_gather(right, "y", YS), axis=1)
    return jnp.concatenate([left, right], axis=-1)


def reduce_slots(terms):
    zs = terms.shape[0]
    cut = cut_of(terms.shape[-1])
    left = ring_reduce([terms[dz, :, :, :cut] for dz in range(zs)], "z")
    left = ring_reduce([left[dy] for dy in range(YS)], "y")
    right = ring_reduce([terms[:, dy, :, cut:] for dy in range(YS)], "y")
    right = ring_reduce([right[dz] for dz in range(zs)], "z")
    return jnp.concatenate([left, right], axis=-1)


def gather_small(rows):
    zs = lax.axis_size("seq") // YS
    block = jnp.stack([rows] + [receive(rows, 0, dy) for dy in range(1, YS)])
    return jnp.stack(ring_gather(block, "z", zs))


def sum_all(value):
    for axis in ("seq", "exp"):
        size = lax.axis_size(axis)
        step = 1
        while step < size:
            value = value + lax.ppermute(value, axis, [(d, d ^ step) for d in range(size)])
            step *= 2
    return value


def three_parts(value):
    high = lax.reduce_precision(value, 8, 7)
    rest = value - high
    middle = lax.reduce_precision(rest, 8, 7)
    low = rest - middle
    return [part.astype(jnp.bfloat16) for part in (high, middle, low)]


def prefix_body(bound_ref, terms_ref, out_ref):
    blocks, rows, lanes = out_ref.shape
    near = lax.broadcasted_iota(jnp.int32, (rows, lanes), 0) < bound_ref[0]
    state = jnp.zeros((rows, lanes), jnp.float32)
    for block in range(blocks):
        out_ref[block] = state.astype(jnp.bfloat16)
        tail = terms_ref[block, rows : rows + 8, :].astype(jnp.float32)
        one = jnp.exp(tail[0:1] + tail[1:2] + tail[2:3])
        two = jnp.exp(tail[3:4] + tail[4:5] + tail[5:6])
        state = state * jnp.where(near, one, two) + terms_ref[block, :rows, :].astype(jnp.float32)


def exclusive_states(own_state, total):
    heads, size, _ = own_state.shape
    count = lax.axis_size("seq")
    place = lax.axis_index("seq")
    pairs = heads // 2
    rows = pairs * size // count
    packed = own_state.reshape(pairs, 2, size, size).transpose(0, 2, 1, 3)
    packed = packed.reshape(count, rows, 2 * size).astype(jnp.bfloat16)
    parts = jnp.stack([p.reshape(pairs, 2) for p in three_parts(total)], axis=1)
    parts = jnp.repeat(parts, size, axis=2)
    starts = np.arange(count) * rows
    near, far = starts // size, (starts + rows - 1) // size
    spare = jnp.zeros((count, 2, 2 * size), jnp.bfloat16)
    payload = jnp.concatenate([packed, parts[near], parts[far], spare], axis=1)
    arrived = lax.all_to_all(payload, "seq", 0, 0, tiled=True)
    bound = ((place * rows) // size + 1) * size - place * rows
    sums = pl.pallas_call(
        prefix_body,
        out_shape=jax.ShapeDtypeStruct((count, rows, 2 * size), jnp.bfloat16),
        in_specs=[
            pl.BlockSpec(memory_space=pltpu.SMEM),
            pl.BlockSpec(memory_space=pltpu.VMEM),
        ],
        out_specs=pl.BlockSpec(memory_space=pltpu.VMEM),
        name="state_prefix",
    )(bound.reshape(1), arrived)
    back = lax.all_to_all(sums, "seq", 0, 0, tiled=True)
    back = back.reshape(pairs, size, 2, size).transpose(0, 2, 1, 3)
    return back.reshape(heads, size, size)


def readout_weights(cumulated, places):
    positions = jnp.arange(cumulated.shape[1], dtype=jnp.int32)
    one_hot = (places[:, None] == positions[None, :]).astype(jnp.float32)
    at_read = jnp.dot(cumulated, one_hot.T, precision=PRECISE)
    allowed = positions[None, :] <= places[:, None]
    exponent = jnp.where(allowed[None], at_read[:, :, None] - cumulated[:, None, :], -1e30)
    return (at_read, jnp.exp(exponent))


def preference_loss(rewards, pair_order, lengths, total_length):
    count = rewards.shape[0]
    ordering = (pair_order[:, None] == jnp.arange(count, dtype=jnp.int32)[None, :]).astype(
        jnp.float32
    )
    ranked = jnp.dot(ordering, rewards, precision=PRECISE).reshape(count // 2, 2)
    fitted = jnp.mean(jax.nn.softplus(ranked[:, 1] - ranked[:, 0]))
    share = lengths.astype(jnp.float32) / total_length
    scatter_breadth = jnp.mean((rewards - jnp.mean(rewards)) * (share - jnp.mean(share)))
    return fitted + LENGTH_WEIGHT * scatter_breadth * scatter_breadth


def per_device(
    resid_rows,
    query_rows,
    key_rows,
    value_rows,
    log_decay,
    read_pos,
    expert_ids,
    pair_order,
    lengths,
    norm_gain,
    router_weight,
    score_weight,
    gate_weight,
    up_weight,
    down_weight,
):
    seq_count = lax.axis_size("seq")
    exp_count = lax.axis_size("exp")
    seq_index = lax.axis_index("seq")
    exp_index = lax.axis_index("exp")
    zs = seq_count // YS
    token_count = key_rows.shape[1]
    model_width = key_rows.shape[2]
    head_count = log_decay.shape[1]
    head_size = model_width // head_count
    read_count = query_rows.shape[1]
    expert_count = router_weight.shape[1]
    capacity = max(2, 4 * read_count // exp_count)
    slot_count = expert_count * capacity
    keys_half = key_rows[0].reshape(token_count, head_count, head_size)
    values_half = value_rows[0].reshape(token_count, head_count, head_size)
    query_half = query_rows[0].reshape(read_count, head_count, head_size)
    query_float = query_half.astype(jnp.float32)
    values_float = values_half.astype(jnp.float32)
    cumulated = jnp.cumsum(log_decay[0], axis=1)
    total = cumulated[:, -1]
    tail_decay = jnp.exp(cumulated[:, -1:] - cumulated).T[:, :, None]
    own_state = jnp.einsum(
        "thi,thj->hij",
        (keys_half.astype(jnp.float32) * tail_decay).astype(jnp.bfloat16),
        values_half,
        preferred_element_type=jnp.float32,
    )
    places = read_pos[0] - seq_index * token_count
    at_read, weight = readout_weights(cumulated, places)
    lift = jnp.exp(at_read).T[:, :, None]

    lifted = (query_float * lift).reshape(read_count, model_width).astype(jnp.bfloat16)
    parts = jnp.stack(three_parts(total) + [jnp.zeros((head_count,), jnp.bfloat16)])
    parts = jnp.pad(parts[:read_count], ((0, 0), (0, LANES - head_count)))
    all_lifted = gather_small(jnp.concatenate([lifted, parts], axis=1))
    all_lifted = all_lifted.reshape(seq_count, read_count, model_width + LANES)

    state_in = exclusive_states(own_state, total)

    query_key = (
        jnp.einsum("rhi,thi->hrt", query_half, keys_half, preferred_element_type=jnp.float32)
        / head_size
    )
    attended = jnp.einsum("hrt,thj->rhj", weight * query_key, values_float, precision=PRECISE)
    attended = (
        attended
        + lift
        * jnp.einsum("rhi,hij->rhj", query_half, state_in, preferred_element_type=jnp.float32)
        / head_size
    )
    residual = resid_rows[0].astype(jnp.float32) + attended.reshape(read_count, model_width)
    inverse = lax.rsqrt(jnp.mean(residual * residual, axis=1, keepdims=True) + EPSILON)
    unit_rows = residual * inverse
    gain_float = norm_gain.astype(jnp.float32)
    normed = (unit_rows * gain_float).astype(jnp.bfloat16)
    logits = jnp.dot(normed, router_weight, preferred_element_type=jnp.float32)
    picks = (
        expert_ids[0][:, :, None] == jnp.arange(expert_count, dtype=jnp.int32)[None, None, :]
    ).astype(jnp.float32)
    chosen = jnp.sum(picks * logits[:, None, :], axis=2)
    first = jax.nn.sigmoid(chosen[:, 0] - chosen[:, 1])
    gates = jnp.stack([first, 1.0 - first], axis=1)
    flat = picks.reshape(read_count * 2, expert_count)
    before = jnp.asarray(np.tril(np.ones((read_count * 2, read_count * 2), np.float32), -1))
    slot_index = jnp.sum(jnp.sum(before[:, :, None] * flat[None], axis=1) * flat, axis=1)
    slot_hot = (slot_index[:, None] == jnp.arange(capacity, dtype=jnp.float32)[None, :]).astype(
        jnp.float32
    )
    placement = (flat[:, :, None] * slot_hot[:, None, :]).reshape(read_count, 2, slot_count)
    by_row = jnp.sum(placement, axis=1)
    gated = jnp.sum(placement * gates[:, :, None], axis=1)
    outgoing = jnp.dot(
        by_row.T.astype(jnp.bfloat16), normed, preferred_element_type=jnp.float32
    ).astype(jnp.bfloat16)
    slot_gate = jnp.sum(gated, axis=0)
    gate_cols = jnp.pad(jnp.stack(three_parts(slot_gate), axis=1), ((0, 0), (0, LANES - 3)))
    outgoing = jnp.concatenate([outgoing, gate_cols], axis=1)
    wide = model_width + LANES
    arrived = lax.all_to_all(
        outgoing.reshape(expert_count, capacity, wide), "exp", 0, 0, tiled=True
    ).reshape(slot_count, wide)
    gathered = gather_slots(arrived).reshape(seq_count * slot_count, wide)

    gate_w = gate_weight[0]
    up_w = up_weight[0]
    down_w = down_weight[0]
    score_float = score_weight.astype(jnp.float32)
    down_score = jnp.sum(down_w.astype(jnp.float32) * score_float[None, :], axis=1)
    piece = gathered[:, :model_width]
    pre_gate = jnp.dot(piece, gate_w, preferred_element_type=jnp.float32)
    pre_up = jnp.dot(piece, up_w, preferred_element_type=jnp.float32)
    gate_sigmoid = jax.nn.sigmoid(pre_gate)
    silu = pre_gate * gate_sigmoid
    slot_score = jnp.sum(silu * pre_up * down_score[None, :], axis=1)
    d_pre_gate = (
        down_score[None, :] * pre_up * gate_sigmoid * (1.0 + pre_gate * (1.0 - gate_sigmoid))
    ).astype(jnp.bfloat16)
    d_pre_up = (down_score[None, :] * silu).astype(jnp.bfloat16)
    back = jnp.einsum("sf,df->sd", d_pre_gate, gate_w, preferred_element_type=jnp.float32)
    back = back + jnp.einsum("sf,df->sd", d_pre_up, up_w, preferred_element_type=jnp.float32)
    score_cols = jnp.pad(slot_score[:, None], ((0, 0), (0, LANES - 1)))
    terms = jnp.concatenate([back, score_cols], axis=1).astype(jnp.bfloat16)
    summed = reduce_slots(terms.reshape(zs, YS, slot_count, wide))

    all_gates = jnp.sum(gathered[:, model_width : model_width + 3].astype(jnp.float32), axis=1)
    share = jnp.sum((all_gates * slot_score).reshape(seq_count, exp_count, capacity), axis=(0, 2))
    own_score = jnp.sum(residual * score_float[None, :])
    share = share + jnp.where(jnp.arange(exp_count) == exp_index, own_score, 0.0)
    rewards = sum_all(share) / (read_count * seq_count)
    pair_loss, d_reward = jax.value_and_grad(preference_loss)(
        rewards, pair_order, lengths, token_count * seq_count
    )
    own_grad = jnp.sum(jnp.where(jnp.arange(exp_count) == exp_index, d_reward, 0.0)) * SCORE_SCALE

    returned = lax.all_to_all(
        summed.reshape(expert_count, capacity, wide), "exp", 0, 0, tiled=True
    ).reshape(slot_count, wide)
    d_in = jnp.dot(gated, returned[:, :model_width].astype(jnp.float32), precision=PRECISE)
    row_score = jnp.sum(
        placement * returned[:, model_width].astype(jnp.float32)[None, None, :], axis=2
    )
    d_logit = (row_score[:, 0] - row_score[:, 1]) * first * (1.0 - first)
    columns = jnp.dot(
        picks[:, 0] - picks[:, 1], router_weight.astype(jnp.float32).T, precision=PRECISE
    )
    d_normed = d_in + d_logit[:, None] * columns
    d_unit = d_normed * gain_float
    slope = score_float[None, :] + inverse * (
        d_unit - unit_rows * jnp.mean(d_unit * unit_rows, axis=1, keepdims=True)
    )
    slope_half = slope.astype(jnp.bfloat16)
    all_slopes = gather_small(slope_half).reshape(seq_count * read_count, head_count, head_size)

    steps = jnp.arange(seq_count, dtype=jnp.int32)
    whose = ((seq_index // YS + steps // YS) % zs) * YS + (seq_index + steps) % YS
    totals = jnp.sum(
        all_lifted[:, :3, model_width : model_width + head_count].astype(jnp.float32), axis=1
    )
    between = ((whose[None, :] > seq_index) & (whose[None, :] < whose[:, None])).astype(jnp.float32)
    reach = jnp.exp(jnp.dot(between, totals, precision=PRECISE))
    reach = jnp.where((whose > seq_index)[:, None], reach, 0.0) / head_size
    far_query = (
        all_lifted[:, :, :model_width]
        .astype(jnp.float32)
        .reshape(seq_count, read_count, head_count, head_size)
        * reach[:, None, :, None]
    ).astype(jnp.bfloat16)
    far_query = far_query.reshape(seq_count * read_count, head_count, head_size)
    suffix = jnp.einsum(
        "rhi,rhj->hij", far_query, all_slopes, preferred_element_type=jnp.float32
    ).astype(jnp.bfloat16)

    d_half = slope_half.reshape(read_count, head_count, head_size)
    grad_dot = (
        jnp.einsum("rhj,thj->hrt", d_half, values_half, preferred_element_type=jnp.float32)
        / head_size
    )
    near_grad = (weight * grad_dot).astype(jnp.bfloat16)
    near_key = (weight * query_key).astype(jnp.bfloat16)
    grad_query = jnp.einsum(
        "hrt,thi->rhi", near_grad, keys_half, preferred_element_type=jnp.float32
    )
    grad_query = (
        grad_query
        + lift
        * jnp.einsum("rhj,hij->rhi", d_half, state_in, preferred_element_type=jnp.float32)
        / head_size
    )
    grad_keys = jnp.einsum(
        "hrt,rhi->thi", near_grad, query_half, preferred_element_type=jnp.float32
    )
    grad_keys = grad_keys + tail_decay * jnp.einsum(
        "hij,thj->thi", suffix, values_half, preferred_element_type=jnp.float32
    )
    grad_values = jnp.einsum("hrt,rhj->thj", near_key, d_half, preferred_element_type=jnp.float32)
    grad_values = grad_values + tail_decay * jnp.einsum(
        "thi,hij->thj", keys_half, suffix, preferred_element_type=jnp.float32
    )
    return (
        pair_loss,
        (own_grad * grad_query).reshape(1, read_count, model_width),
        (own_grad * slope).reshape(1, read_count, model_width),
        (own_grad * grad_keys).reshape(1, token_count, model_width).astype(jnp.bfloat16),
        (own_grad * grad_values).reshape(1, token_count, model_width).astype(jnp.bfloat16),
    )


def solution(mesh):
    in_specs = (
        P("exp", "seq", None),
        P("exp", "seq", None),
        P("exp", "seq", None),
        P("exp", "seq", None),
        P("exp", None, "seq"),
        P("exp", "seq"),
        P("exp", "seq", None),
        P(),
        P(),
        P(),
        P(),
        P(),
        P("exp", None, "seq"),
        P("exp", None, "seq"),
        P("exp", "seq", None),
    )
    out_specs = (
        P(),
        P("exp", "seq", None),
        P("exp", "seq", None),
        P("exp", "seq", None),
        P("exp", "seq", None),
    )
    return jax.shard_map(
        per_device, mesh=mesh, in_specs=in_specs, out_specs=out_specs, check_vma=False
    )
```

```python
import jax
import jax.numpy as jnp
import numpy as np
from jax import lax
from jax.experimental import pallas as pl
from jax.experimental.pallas import tpu as pltpu
from jax.sharding import PartitionSpec as P

PRECISE = lax.Precision.HIGHEST
EPSILON = 1e-06
LENGTH_WEIGHT = 4.0
SCORE_SCALE = 256.0
YS = 4
LANES = 128


def receive(value, dz, dy):
    zs = lax.axis_size("seq") // YS
    pairs = [
        (((z + dz) % zs) * YS + (y + dy) % YS, z * YS + y) for z in range(zs) for y in range(YS)
    ]
    return lax.ppermute(value, "seq", pairs)


def split_cols(value):
    half = -(-value.shape[-1] // (2 * LANES)) * LANES
    return value[..., :half], value[..., half:]


def shifted(axis):
    if axis == "z":
        return lambda value, step: receive(value, step, 0)
    return lambda value, step: receive(value, 0, step)


def direct_gather(own, axis, count):
    get = shifted(axis)
    return [own] + [get(own, step if step <= count // 2 else step - count) for step in range(1, count)]


def ring_gather(own, axis, count, halves):
    get = shifted(axis)
    blocks = [None] * count
    blocks[0] = own
    ahead = behind = own
    for lap in range(1, count // 2):
        ahead, behind = get(ahead, 1), get(behind, -1)
        blocks[lap], blocks[count - lap] = ahead, behind
    if halves:
        first, _ = split_cols(ahead)
        _, second = split_cols(behind)
        blocks[count // 2] = jnp.concatenate([get(first, 1), get(second, -1)], axis=-1)
    else:
        blocks[count // 2] = get(ahead, 1)
    return blocks


def add_rounded(left, right):
    return (left.astype(jnp.float32) + right.astype(jnp.float32)).astype(jnp.bfloat16)


def direct_reduce(blocks, axis):
    get = shifted(axis)
    count = len(blocks)
    total = blocks[0].astype(jnp.float32)
    for step in range(1, count):
        total = total + get(
            blocks[step], -step if step <= count // 2 else count - step
        ).astype(jnp.float32)
    return total.astype(jnp.bfloat16)


def ring_reduce(blocks, axis, halves):
    get = shifted(axis)
    count = len(blocks)
    middle = count // 2
    blocks = list(blocks)
    if halves:
        first, second = split_cols(blocks[middle])
        first, second = get(first, -1), get(second, 1)
        half = first.shape[-1]
        up, down = blocks[middle - 1], blocks[middle + 1]
        blocks[middle - 1] = jnp.concatenate(
            [add_rounded(up[..., :half], first), up[..., half:]], axis=-1
        )
        blocks[middle + 1] = jnp.concatenate(
            [down[..., :half], add_rounded(down[..., half:], second)], axis=-1
        )
    else:
        blocks[middle - 1] = add_rounded(blocks[middle - 1], get(blocks[middle], -1))
    first, second = blocks[middle - 1], blocks[middle + 1]
    for lap in range(middle - 1, 0, -1):
        first, second = get(first, -1), get(second, 1)
        if lap > 1:
            first = add_rounded(blocks[lap - 1], first)
            second = add_rounded(blocks[count - lap + 1], second)
    total = (
        blocks[0].astype(jnp.float32) + first.astype(jnp.float32) + second.astype(jnp.float32)
    )
    return total.astype(jnp.bfloat16)


def cut_of(width):
    return -(-width // (2 * LANES)) * LANES


def gather_slots(rows):
    zs = lax.axis_size("seq") // YS
    cut = cut_of(rows.shape[-1])
    right = jnp.stack(direct_gather(rows[:, cut:], "z", zs))
    left = jnp.stack(direct_gather(rows[:, :cut], "y", YS))
    left = jnp.stack(ring_gather(left, "z", zs, False))
    right = jnp.stack(ring_gather(right, "y", YS, True), axis=1)
    return jnp.concatenate([left, right], axis=-1)


def reduce_slots(terms):
    zs = terms.shape[0]
    cut = cut_of(terms.shape[-1])
    left = ring_reduce([terms[dz, :, :, :cut] for dz in range(zs)], "z", False)
    right = ring_reduce([terms[:, dy, :, cut:] for dy in range(YS)], "y", True)
    left = direct_reduce([left[dy] for dy in range(YS)], "y")
    right = direct_reduce([right[dz] for dz in range(zs)], "z")
    return jnp.concatenate([left, right], axis=-1)


def gather_small(rows, after=None):
    zs = lax.axis_size("seq") // YS
    block = jnp.stack(direct_gather(rows, "y", YS))
    if after is not None:
        block, _ = lax.optimization_barrier((block, after))
    return jnp.stack(ring_gather(block, "z", zs, False))


def exchange_scalars(value):
    size = lax.axis_size("exp")
    place = lax.axis_index("exp")
    order = jnp.arange(size)
    value = value.reshape(1)
    out = jnp.where(order == place, value, 0.0)
    for step in range(1, size):
        other = lax.ppermute(value, "exp", [(d, d ^ step) for d in range(size)])
        out = out + jnp.where(order == place ^ step, other, 0.0)
    return out


def three_parts(value):
    high = lax.reduce_precision(value, 8, 7)
    rest = value - high
    middle = lax.reduce_precision(rest, 8, 7)
    low = rest - middle
    return [part.astype(jnp.bfloat16) for part in (high, middle, low)]


def prefix_body(bound_ref, terms_ref, out_ref):
    blocks, rows, lanes = out_ref.shape
    near = lax.broadcasted_iota(jnp.int32, (rows, lanes), 0) < bound_ref[0]
    state = jnp.zeros((rows, lanes), jnp.float32)
    for block in range(blocks):
        out_ref[block] = state.astype(jnp.bfloat16)
        tail = terms_ref[block, rows : rows + 8, :].astype(jnp.float32)
        one = jnp.exp(tail[0:1] + tail[1:2] + tail[2:3])
        two = jnp.exp(tail[3:4] + tail[4:5] + tail[5:6])
        state = state * jnp.where(near, one, two) + terms_ref[block, :rows, :].astype(jnp.float32)


def exclusive_states(own_state, total):
    heads, size, _ = own_state.shape
    count = lax.axis_size("seq")
    place = lax.axis_index("seq")
    pairs = heads // 2
    rows = pairs * size // count
    packed = own_state.reshape(pairs, 2, size, size).transpose(0, 2, 1, 3)
    packed = packed.reshape(count, rows, 2 * size).astype(jnp.bfloat16)
    parts = jnp.stack([p.reshape(pairs, 2) for p in three_parts(total)], axis=1)
    parts = jnp.repeat(parts, size, axis=2)
    starts = np.arange(count) * rows
    near, far = starts // size, (starts + rows - 1) // size
    spare = jnp.zeros((count, 2, 2 * size), jnp.bfloat16)
    payload = jnp.concatenate([packed, parts[near], parts[far], spare], axis=1)
    arrived = lax.all_to_all(payload, "seq", 0, 0, tiled=True)
    bound = ((place * rows) // size + 1) * size - place * rows
    sums = pl.pallas_call(
        prefix_body,
        out_shape=jax.ShapeDtypeStruct((count, rows, 2 * size), jnp.bfloat16),
        in_specs=[
            pl.BlockSpec(memory_space=pltpu.SMEM),
            pl.BlockSpec(memory_space=pltpu.VMEM),
        ],
        out_specs=pl.BlockSpec(memory_space=pltpu.VMEM),
        name="state_prefix",
    )(bound.reshape(1), arrived)
    back = lax.all_to_all(sums, "seq", 0, 0, tiled=True)
    back = back.reshape(pairs, size, 2, size).transpose(0, 2, 1, 3)
    return back.reshape(heads, size, size), arrived


def readout_weights(cumulated, places):
    positions = jnp.arange(cumulated.shape[1], dtype=jnp.int32)
    one_hot = (places[:, None] == positions[None, :]).astype(jnp.float32)
    at_read = jnp.dot(cumulated, one_hot.T, precision=PRECISE)
    allowed = positions[None, :] <= places[:, None]
    exponent = jnp.where(allowed[None], at_read[:, :, None] - cumulated[:, None, :], -1e30)
    return (at_read, jnp.exp(exponent))


def preference_loss(rewards, pair_order, lengths, total_length):
    count = rewards.shape[0]
    ordering = (pair_order[:, None] == jnp.arange(count, dtype=jnp.int32)[None, :]).astype(
        jnp.float32
    )
    ranked = jnp.dot(ordering, rewards, precision=PRECISE).reshape(count // 2, 2)
    fitted = jnp.mean(jax.nn.softplus(ranked[:, 1] - ranked[:, 0]))
    share = lengths.astype(jnp.float32) / total_length
    scatter_breadth = jnp.mean((rewards - jnp.mean(rewards)) * (share - jnp.mean(share)))
    return fitted + LENGTH_WEIGHT * scatter_breadth * scatter_breadth


def per_device(
    resid_rows,
    query_rows,
    key_rows,
    value_rows,
    log_decay,
    read_pos,
    expert_ids,
    pair_order,
    lengths,
    norm_gain,
    router_weight,
    score_weight,
    gate_weight,
    up_weight,
    down_weight,
):
    seq_count = lax.axis_size("seq")
    exp_count = lax.axis_size("exp")
    seq_index = lax.axis_index("seq")
    exp_index = lax.axis_index("exp")
    zs = seq_count // YS
    token_count = key_rows.shape[1]
    model_width = key_rows.shape[2]
    head_count = log_decay.shape[1]
    head_size = model_width // head_count
    read_count = query_rows.shape[1]
    expert_count = router_weight.shape[1]
    capacity = max(2, 4 * read_count // exp_count)
    slot_count = expert_count * capacity
    keys_half = key_rows[0].reshape(token_count, head_count, head_size)
    values_half = value_rows[0].reshape(token_count, head_count, head_size)
    query_half = query_rows[0].reshape(read_count, head_count, head_size)
    query_float = query_half.astype(jnp.float32)
    values_float = values_half.astype(jnp.float32)
    cumulated = jnp.cumsum(log_decay[0], axis=1)
    total = cumulated[:, -1]
    tail_decay = jnp.exp(cumulated[:, -1:] - cumulated).T[:, :, None]
    own_state = jnp.einsum(
        "thi,thj->hij",
        (keys_half.astype(jnp.float32) * tail_decay).astype(jnp.bfloat16),
        values_half,
        preferred_element_type=jnp.float32,
    )
    places = read_pos[0] - seq_index * token_count
    at_read, weight = readout_weights(cumulated, places)
    lift = jnp.exp(at_read).T[:, :, None]

    lifted = (query_float * lift).reshape(read_count, model_width).astype(jnp.bfloat16)
    parts = jnp.stack(three_parts(total) + [jnp.zeros((head_count,), jnp.bfloat16)])
    parts = jnp.pad(parts[:read_count], ((0, 0), (0, LANES - head_count)))
    state_in, arrived_states = exclusive_states(own_state, total)
    all_lifted = gather_small(jnp.concatenate([lifted, parts], axis=1), arrived_states)
    all_lifted = all_lifted.reshape(seq_count, read_count, model_width + LANES)

    query_key = (
        jnp.einsum("rhi,thi->hrt", query_half, keys_half, preferred_element_type=jnp.float32)
        / head_size
    )
    attended = jnp.einsum("hrt,thj->rhj", weight * query_key, values_float, precision=PRECISE)
    attended = (
        attended
        + lift
        * jnp.einsum("rhi,hij->rhj", query_half, state_in, preferred_element_type=jnp.float32)
        / head_size
    )
    residual = resid_rows[0].astype(jnp.float32) + attended.reshape(read_count, model_width)
    inverse = lax.rsqrt(jnp.mean(residual * residual, axis=1, keepdims=True) + EPSILON)
    unit_rows = residual * inverse
    gain_float = norm_gain.astype(jnp.float32)
    normed = (unit_rows * gain_float).astype(jnp.bfloat16)
    logits = jnp.dot(normed, router_weight, preferred_element_type=jnp.float32)
    picks = (
        expert_ids[0][:, :, None] == jnp.arange(expert_count, dtype=jnp.int32)[None, None, :]
    ).astype(jnp.float32)
    chosen = jnp.sum(picks * logits[:, None, :], axis=2)
    first = jax.nn.sigmoid(chosen[:, 0] - chosen[:, 1])
    gates = jnp.stack([first, 1.0 - first], axis=1)
    flat = picks.reshape(read_count * 2, expert_count)
    before = jnp.asarray(np.tril(np.ones((read_count * 2, read_count * 2), np.float32), -1))
    slot_index = jnp.sum(jnp.sum(before[:, :, None] * flat[None], axis=1) * flat, axis=1)
    slot_hot = (slot_index[:, None] == jnp.arange(capacity, dtype=jnp.float32)[None, :]).astype(
        jnp.float32
    )
    placement = (flat[:, :, None] * slot_hot[:, None, :]).reshape(read_count, 2, slot_count)
    by_row = jnp.sum(placement, axis=1)
    gated = jnp.sum(placement * gates[:, :, None], axis=1)
    outgoing = jnp.dot(
        by_row.T.astype(jnp.bfloat16), normed, preferred_element_type=jnp.float32
    ).astype(jnp.bfloat16)
    wide = model_width + LANES
    arrived = lax.all_to_all(
        outgoing.reshape(expert_count, capacity, model_width), "exp", 0, 0, tiled=True
    ).reshape(slot_count, model_width)
    piece = gather_slots(arrived).reshape(seq_count * slot_count, model_width)

    gate_w = gate_weight[0]
    up_w = up_weight[0]
    down_w = down_weight[0]
    score_float = score_weight.astype(jnp.float32)
    down_score = jnp.sum(down_w.astype(jnp.float32) * score_float[None, :], axis=1)
    pre_gate = jnp.dot(piece, gate_w, preferred_element_type=jnp.float32)
    pre_up = jnp.dot(piece, up_w, preferred_element_type=jnp.float32)
    gate_sigmoid = jax.nn.sigmoid(pre_gate)
    silu = pre_gate * gate_sigmoid
    slot_score = jnp.sum(silu * pre_up * down_score[None, :], axis=1)
    d_pre_gate = (
        down_score[None, :] * pre_up * gate_sigmoid * (1.0 + pre_gate * (1.0 - gate_sigmoid))
    ).astype(jnp.bfloat16)
    d_pre_up = (down_score[None, :] * silu).astype(jnp.bfloat16)
    back = jnp.einsum("sf,df->sd", d_pre_gate, gate_w, preferred_element_type=jnp.float32)
    back = back + jnp.einsum("sf,df->sd", d_pre_up, up_w, preferred_element_type=jnp.float32)
    score_cols = jnp.pad(slot_score[:, None], ((0, 0), (0, LANES - 1)))
    terms = jnp.concatenate([back, score_cols], axis=1).astype(jnp.bfloat16)
    summed = reduce_slots(terms.reshape(zs, YS, slot_count, wide))

    returned = lax.all_to_all(
        summed.reshape(expert_count, capacity, wide), "exp", 0, 0, tiled=True
    ).reshape(slot_count, wide)
    d_in = jnp.dot(gated, returned[:, :model_width].astype(jnp.float32), precision=PRECISE)
    row_score = jnp.sum(
        placement * returned[:, model_width].astype(jnp.float32)[None, None, :], axis=2
    )
    d_logit = (row_score[:, 0] - row_score[:, 1]) * first * (1.0 - first)
    columns = jnp.dot(
        picks[:, 0] - picks[:, 1], router_weight.astype(jnp.float32).T, precision=PRECISE
    )
    d_normed = d_in + d_logit[:, None] * columns
    d_unit = d_normed * gain_float
    slope = score_float[None, :] + inverse * (
        d_unit - unit_rows * jnp.mean(d_unit * unit_rows, axis=1, keepdims=True)
    )
    slope_half = slope.astype(jnp.bfloat16)

    own_score = jnp.sum(residual * score_float[None, :]) + jnp.sum(gates * row_score)
    own_score = jnp.pad(jnp.stack(three_parts(own_score)).reshape(1, 3), ((0, 0), (0, LANES - 3)))
    own_score = jnp.broadcast_to(own_score, (read_count, LANES))
    all_slopes = gather_small(jnp.concatenate([slope_half, own_score], axis=1))
    all_slopes = all_slopes.reshape(seq_count, read_count, wide)

    steps = jnp.arange(seq_count, dtype=jnp.int32)
    whose = ((seq_index // YS + steps // YS) % zs) * YS + (seq_index + steps) % YS
    shares = jnp.sum(all_slopes[:, 0, model_width : model_width + 3].astype(jnp.float32), axis=1)
    shares = jnp.sum(jnp.where(whose[:, None] == steps[None, :], shares[:, None], 0.0), axis=0)
    shares = lax.optimization_barrier(shares)
    rewards = exchange_scalars(jnp.sum(shares) / (read_count * seq_count))
    pair_loss, d_reward = jax.value_and_grad(preference_loss)(
        rewards, pair_order, lengths, token_count * seq_count
    )
    own_grad = jnp.sum(jnp.where(jnp.arange(exp_count) == exp_index, d_reward, 0.0)) * SCORE_SCALE
    all_slopes = all_slopes[:, :, :model_width].reshape(
        seq_count * read_count, head_count, head_size
    )
    totals = jnp.sum(
        all_lifted[:, :3, model_width : model_width + head_count].astype(jnp.float32), axis=1
    )
    between = ((whose[None, :] > seq_index) & (whose[None, :] < whose[:, None])).astype(jnp.float32)
    reach = jnp.exp(jnp.dot(between, totals, precision=PRECISE))
    reach = jnp.where((whose > seq_index)[:, None], reach, 0.0) / head_size
    far_query = (
        all_lifted[:, :, :model_width]
        .astype(jnp.float32)
        .reshape(seq_count, read_count, head_count, head_size)
        * reach[:, None, :, None]
    ).astype(jnp.bfloat16)
    far_query = far_query.reshape(seq_count * read_count, head_count, head_size)
    suffix = jnp.einsum(
        "rhi,rhj->hij", far_query, all_slopes, preferred_element_type=jnp.float32
    ).astype(jnp.bfloat16)

    d_half = slope_half.reshape(read_count, head_count, head_size)
    grad_dot = (
        jnp.einsum("rhj,thj->hrt", d_half, values_half, preferred_element_type=jnp.float32)
        / head_size
    )
    near_grad = (weight * grad_dot).astype(jnp.bfloat16)
    near_key = (weight * query_key).astype(jnp.bfloat16)
    grad_query = jnp.einsum(
        "hrt,thi->rhi", near_grad, keys_half, preferred_element_type=jnp.float32
    )
    grad_query = (
        grad_query
        + lift
        * jnp.einsum("rhj,hij->rhi", d_half, state_in, preferred_element_type=jnp.float32)
        / head_size
    )
    grad_keys = jnp.einsum(
        "hrt,rhi->thi", near_grad, query_half, preferred_element_type=jnp.float32
    )
    grad_keys = grad_keys + tail_decay * jnp.einsum(
        "hij,thj->thi", suffix, values_half, preferred_element_type=jnp.float32
    )
    grad_values = jnp.einsum("hrt,rhj->thj", near_key, d_half, preferred_element_type=jnp.float32)
    grad_values = grad_values + tail_decay * jnp.einsum(
        "thi,hij->thj", keys_half, suffix, preferred_element_type=jnp.float32
    )
    return (
        pair_loss,
        (own_grad * grad_query).reshape(1, read_count, model_width),
        (own_grad * slope).reshape(1, read_count, model_width),
        (own_grad * grad_keys).reshape(1, token_count, model_width).astype(jnp.bfloat16),
        (own_grad * grad_values).reshape(1, token_count, model_width).astype(jnp.bfloat16),
    )


def solution(mesh):
    in_specs = (
        P("exp", "seq", None),
        P("exp", "seq", None),
        P("exp", "seq", None),
        P("exp", "seq", None),
        P("exp", None, "seq"),
        P("exp", "seq"),
        P("exp", "seq", None),
        P(),
        P(),
        P(),
        P(),
        P(),
        P("exp", None, "seq"),
        P("exp", None, "seq"),
        P("exp", "seq", None),
    )
    out_specs = (
        P(),
        P("exp", "seq", None),
        P("exp", "seq", None),
        P("exp", "seq", None),
        P("exp", "seq", None),
    )
    return jax.shard_map(
        per_device, mesh=mesh, in_specs=in_specs, out_specs=out_specs, check_vma=False
    )
```

```python
import functools

import jax
import jax.numpy as jnp
import numpy as np
from jax import lax
from jax.experimental import pallas as pl
from jax.experimental.pallas import tpu as pltpu
from jax.sharding import PartitionSpec as P

EPSILON = 1e-06
LENGTH_WEIGHT = 4.0
SCORE_SCALE = 256.0
YS = 4
LANES = 128


def receive(value, dz, dy):
    zs = lax.axis_size("seq") // YS
    pairs = [
        (((z + dz) % zs) * YS + (y + dy) % YS, z * YS + y) for z in range(zs) for y in range(YS)
    ]
    return lax.ppermute(value, "seq", pairs)


def split_cols(value):
    half = -(-value.shape[-1] // (2 * LANES)) * LANES
    return value[..., :half], value[..., half:]


def shifted(axis):
    if axis == "z":
        return lambda value, step: receive(value, step, 0)
    return lambda value, step: receive(value, 0, step)


def direct_gather(own, axis, count):
    get = shifted(axis)
    return [own] + [get(own, step if step <= count // 2 else step - count) for step in range(1, count)]


def ring_gather(own, axis, count, halves):
    get = shifted(axis)
    blocks = [None] * count
    blocks[0] = own
    ahead = behind = own
    for lap in range(1, count // 2):
        ahead, behind = get(ahead, 1), get(behind, -1)
        blocks[lap], blocks[count - lap] = ahead, behind
    if halves:
        first, _ = split_cols(ahead)
        _, second = split_cols(behind)
        blocks[count // 2] = jnp.concatenate([get(first, 1), get(second, -1)], axis=-1)
    else:
        blocks[count // 2] = get(ahead, 1)
    return blocks


def add_rounded(left, right):
    return (left.astype(jnp.float32) + right.astype(jnp.float32)).astype(jnp.bfloat16)


def direct_reduce(blocks, axis):
    get = shifted(axis)
    count = len(blocks)
    total = blocks[0].astype(jnp.float32)
    for step in range(1, count):
        total = total + get(
            blocks[step], -step if step <= count // 2 else count - step
        ).astype(jnp.float32)
    return total.astype(jnp.bfloat16)


def ring_reduce(blocks, axis, halves):
    get = shifted(axis)
    count = len(blocks)
    middle = count // 2
    blocks = list(blocks)
    if halves:
        first, second = split_cols(blocks[middle])
        first, second = get(first, -1), get(second, 1)
        half = first.shape[-1]
        up, down = blocks[middle - 1], blocks[middle + 1]
        blocks[middle - 1] = jnp.concatenate(
            [add_rounded(up[..., :half], first), up[..., half:]], axis=-1
        )
        blocks[middle + 1] = jnp.concatenate(
            [down[..., :half], add_rounded(down[..., half:], second)], axis=-1
        )
    else:
        blocks[middle - 1] = add_rounded(blocks[middle - 1], get(blocks[middle], -1))
    first, second = blocks[middle - 1], blocks[middle + 1]
    for lap in range(middle - 1, 0, -1):
        first, second = get(first, -1), get(second, 1)
        if lap > 1:
            first = add_rounded(blocks[lap - 1], first)
            second = add_rounded(blocks[count - lap + 1], second)
    total = (
        blocks[0].astype(jnp.float32) + first.astype(jnp.float32) + second.astype(jnp.float32)
    )
    return total.astype(jnp.bfloat16)


def cut_of(width):
    return -(-width // (2 * LANES)) * LANES


def gather_slots(rows):
    zs = lax.axis_size("seq") // YS
    cut = cut_of(rows.shape[-1])
    right = jnp.stack(direct_gather(rows[:, cut:], "z", zs))
    left = jnp.stack(direct_gather(rows[:, :cut], "y", YS))
    left = jnp.stack(ring_gather(left, "z", zs, False))
    right = jnp.stack(ring_gather(right, "y", YS, True), axis=1)
    return jnp.concatenate([left, right], axis=-1)


def reduce_slots(terms):
    zs = terms.shape[0]
    cut = cut_of(terms.shape[-1])
    left = ring_reduce([terms[dz, :, :, :cut] for dz in range(zs)], "z", False)
    right = ring_reduce([terms[:, dy, :, cut:] for dy in range(YS)], "y", True)
    left = direct_reduce([left[dy] for dy in range(YS)], "y")
    right = direct_reduce([right[dz] for dz in range(zs)], "z")
    return jnp.concatenate([left, right], axis=-1)


def gather_small(rows):
    zs = lax.axis_size("seq") // YS
    block = jnp.stack(direct_gather(rows, "y", YS))
    return jnp.stack(ring_gather(block, "z", zs, False))


F32 = jnp.float32
BF16 = jnp.bfloat16

NT = (((1,), (1,)), ((), ()))
TN = (((0,), (0,)), ((), ()))
NN = (((1,), (0,)), ((), ()))


def mm(left, right, dims=NN):
    return lax.dot_general(left, right, dims, preferred_element_type=F32)


def parts_of(value):
    high = value.astype(BF16).astype(F32)
    middle = (value - high).astype(BF16).astype(F32)
    return high, middle, (value - high - middle).astype(BF16).astype(F32)


def by_half(left, right, low):
    return jnp.where(low, left, right)


def both_rows(rows, low):
    zero = jnp.zeros_like(rows)
    return jnp.concatenate([jnp.where(low, rows, zero), jnp.where(low, zero, rows)], axis=0)


def prepare_body(
    places_ref, keys_ref, values_ref, query_ref, decay_ref,
    payload_ref, lifted_ref, total_ref, tails_ref, lifts_ref, weights_ref, scores_ref, attended_ref, spread_ref,
):
    tokens, width = keys_ref.shape
    reads = query_ref.shape[0]
    heads = decay_ref.shape[0]
    pairs = heads // 2
    size = width // heads
    blocks, _, _ = payload_ref.shape
    rows = pairs * size // blocks
    decay = decay_ref[...]
    t0 = lax.broadcasted_iota(jnp.int32, (tokens, tokens), 0)
    t1 = lax.broadcasted_iota(jnp.int32, (tokens, tokens), 1)
    lower = (t1 <= t0).astype(F32)
    upper = (t0 <= t1).astype(F32)
    cum = sum(mm(part.astype(BF16), upper.astype(BF16)) for part in parts_of(decay))
    cum_t = sum(mm(lower.astype(BF16), part.astype(BF16), NT) for part in parts_of(decay))
    spread_ref[...] = cum_t
    total_ref[...] = cum_t[tokens - 1 : tokens]
    tail = jnp.exp(cum_t[tokens - 1 : tokens] - cum_t)
    tails_ref[...] = tail
    total = cum[:, tokens - 1 : tokens]
    at_read = jnp.concatenate([spread_ref[pl.ds(places_ref[r], 1), :] for r in range(reads)], axis=0)
    lift = jnp.exp(at_read)
    lifts_ref[...] = lift
    lane = lax.broadcasted_iota(jnp.int32, (1, LANES), 1)
    low = lane < size
    spot = lax.broadcasted_iota(jnp.int32, (reads, tokens), 1)
    row = lax.broadcasted_iota(jnp.int32, (reads, tokens), 0)
    place = jnp.zeros((reads, tokens), jnp.int32)
    for r in range(reads):
        place = jnp.where(row == r, places_ref[r], place)
    allowed = spot <= place
    lanes_total = []
    for p in range(pairs):
        cols = slice(p * LANES, (p + 1) * LANES)
        one, two = 2 * p, 2 * p + 1
        key, value, query = keys_ref[:, cols], values_ref[:, cols], query_ref[:, cols]
        fade = by_half(tail[:, one : one + 1], tail[:, two : two + 1], low)
        state = mm((key.astype(F32) * fade).astype(BF16), value, TN)
        state = by_half(state[:size], state[size:], low).astype(BF16)
        for chunk in range(size // 16):
            where = p * (size // 16) + chunk
            block, offset = where // (rows // 16), where % (rows // 16)
            payload_ref[block, offset * 16 : offset * 16 + 16, :] = state[chunk * 16 : chunk * 16 + 16]
        lanes_total.append(by_half(total[one : one + 1], total[two : two + 1], low))
        raised = by_half(lift[:, one : one + 1], lift[:, two : two + 1], low)
        lifted_ref[:, cols] = (query.astype(F32) * raised).astype(BF16)
        weight = [
            jnp.exp(jnp.where(allowed, at_read[:, h : h + 1] - cum[h : h + 1, :], -1e30))
            for h in (one, two)
        ]
        weight = jnp.concatenate(weight, axis=0)
        weights_ref[p] = weight
        score = weight * mm(both_rows(query, low), key, NT) * (1.0 / size)
        scores_ref[p] = score
        near = mm(score.astype(BF16), value)
        attended_ref[:, cols] = by_half(near[:reads], near[reads:], low)
    for block in range(blocks):
        first = block * rows // size
        last = (block * rows + rows - 1) // size
        meta = list(parts_of(lanes_total[first])) + list(parts_of(lanes_total[last]))
        meta = jnp.concatenate(meta + [jnp.zeros((2, LANES), F32)], axis=0)
        payload_ref[block, rows : rows + 8, :] = meta.astype(BF16)


def prepare(places, keys, values, query, decay, blocks):
    tokens, width = keys.shape
    reads = query.shape[0]
    heads = decay.shape[0]
    pairs = heads // 2
    rows = pairs * (width // heads) // blocks
    vmem = pl.BlockSpec(memory_space=pltpu.VMEM)
    return pl.pallas_call(
        prepare_body,
        out_shape=(
            jax.ShapeDtypeStruct((blocks, rows + 8, LANES), BF16),
            jax.ShapeDtypeStruct((reads, width), BF16),
            jax.ShapeDtypeStruct((1, heads), F32),
            jax.ShapeDtypeStruct((tokens, heads), F32),
            jax.ShapeDtypeStruct((reads, heads), F32),
            jax.ShapeDtypeStruct((pairs, 2 * reads, tokens), F32),
            jax.ShapeDtypeStruct((pairs, 2 * reads, tokens), F32),
            jax.ShapeDtypeStruct((reads, width), F32),
        ),
        in_specs=[pl.BlockSpec(memory_space=pltpu.SMEM)] + [vmem] * 4,
        out_specs=(vmem,) * 8,
        scratch_shapes=[pltpu.VMEM((tokens, heads), F32)],
        name="prepare",
    )(places, keys, values, query, decay)


def finish_body(
    place_ref, keys_ref, values_ref, query_ref, slope_ref, far_ref, parts_ref, state_ref, tails_ref,
    lifts_ref, weights_ref, scores_ref,
    keys_out, values_out, query_out,
):
    tokens, width = keys_ref.shape
    reads = query_ref.shape[0]
    heads = tails_ref.shape[1]
    pairs = heads // 2
    size = width // heads
    low = lax.broadcasted_iota(jnp.int32, (1, LANES), 1) < size
    r0 = lax.broadcasted_iota(jnp.int32, (LANES, LANES), 0) < size
    r1 = lax.broadcasted_iota(jnp.int32, (LANES, LANES), 1) < size
    same = r0 == r1
    tail, lift = tails_ref[...], lifts_ref[...]
    own, ys = place_ref[0], place_ref[1]
    count, blocks = far_ref.shape[0], parts_ref.shape[1]

    def whose(step):
        return ((own // ys + step // ys) % (blocks // ys)) * ys + (own + step) % ys

    row = lax.broadcasted_iota(jnp.int32, (count, blocks), 0)
    other = whose(lax.broadcasted_iota(jnp.int32, (count, blocks), 1))
    mine = whose(row // (2 * reads))
    between = ((other > own) & (other < mine)).astype(BF16)
    reach = jnp.exp(mm(between, parts_ref[0]) + mm(between, parts_ref[1]) + mm(between, parts_ref[2]))
    later = (mine[:, :1] > own) & (row[:, :1] % (2 * reads) < reads)
    reach = jnp.where(later, reach, 0.0) * (1.0 / size)
    for p in range(pairs):
        cols = slice(p * LANES, (p + 1) * LANES)
        one, two = 2 * p, 2 * p + 1
        key, value, query = keys_ref[:, cols], values_ref[:, cols], query_ref[:, cols]
        slope = slope_ref[:, cols].astype(BF16)
        far = by_half(reach[:, one : one + 1], reach[:, two : two + 1], low)
        rows = far_ref[:, cols]
        far = (pltpu.roll(rows.astype(F32), count - reads, 0) * far).astype(BF16)
        suffix = jnp.where(same, mm(far, rows, TN), 0.0).astype(BF16)
        fade = by_half(tail[:, one : one + 1], tail[:, two : two + 1], low)
        slopes = both_rows(slope, low)
        near = (weights_ref[p] * mm(slopes, value, NT) * (1.0 / size)).astype(BF16)
        keys_out[:, cols] = mm(near, both_rows(query, low), TN) + fade * mm(value, suffix, NT)
        values_out[:, cols] = mm(scores_ref[p].astype(BF16), slopes, TN) + fade * mm(key, suffix)
        state = state_ref[p]
        zero = jnp.zeros_like(state)
        state = jnp.concatenate([jnp.where(low, state, zero), jnp.where(low, zero, state)], axis=0)
        raised = by_half(lift[:, one : one + 1], lift[:, two : two + 1], low) * (1.0 / size)
        own = mm(near, key)
        query_out[:, cols] = by_half(own[:reads], own[reads:], low) + raised * mm(slope, state, NT)


def finish(place, keys, values, query, slope, far, parts, state, tails, lifts, weights, scores):
    tokens, width = keys.shape
    reads = query.shape[0]
    vmem = pl.BlockSpec(memory_space=pltpu.VMEM)
    return pl.pallas_call(
        finish_body,
        out_shape=(
            jax.ShapeDtypeStruct((tokens, width), F32),
            jax.ShapeDtypeStruct((tokens, width), F32),
            jax.ShapeDtypeStruct((reads, width), F32),
        ),
        in_specs=[pl.BlockSpec(memory_space=pltpu.SMEM)] + [vmem] * 11,
        out_specs=(vmem,) * 3,
        name="finish",
    )(place, keys, values, query, slope, far, parts, state, tails, lifts, weights, scores)


def targets(ids_ref, capacity):
    reads = ids_ref.shape[0]
    out = []
    for r in range(reads):
        mine = []
        for k in range(2):
            name = ids_ref[r, k]
            slot = name * capacity
            for q in range(r):
                slot = slot + (ids_ref[q, 0] == name).astype(jnp.int32)
                slot = slot + (ids_ref[q, 1] == name).astype(jnp.int32)
            mine.append(slot)
        out.append(mine)
    return out


def column(scalars):
    rows = lax.broadcasted_iota(jnp.int32, (len(scalars), 1), 0)
    out = jnp.zeros((len(scalars), 1), jnp.int32)
    for r, scalar in enumerate(scalars):
        out = jnp.where(rows == r, scalar, out)
    return out


def route_body(
    ids_ref, state_ref, query_ref, lifts_ref, attended_ref, resid_ref, gain_ref, router_ref, score_ref,
    out_ref, unit_ref, small_ref, residual_ref,
):
    reads, width = query_ref.shape
    heads = lifts_ref.shape[1]
    pairs = heads // 2
    size = width // heads
    slots = out_ref.shape[0]
    experts = router_ref.shape[0]
    capacity = slots // experts
    low = lax.broadcasted_iota(jnp.int32, (1, LANES), 1) < size
    lift = lifts_ref[...]
    square = jnp.zeros((reads, LANES), F32)
    for p in range(pairs):
        cols = slice(p * LANES, (p + 1) * LANES)
        one, two = 2 * p, 2 * p + 1
        state = state_ref[p]
        zero = jnp.zeros_like(state)
        state = jnp.concatenate([jnp.where(low, state, zero), jnp.where(low, zero, state)], axis=0)
        raised = by_half(lift[:, one : one + 1], lift[:, two : two + 1], low) * (1.0 / size)
        residual = (
            resid_ref[:, cols].astype(F32) + attended_ref[:, cols] + raised * mm(query_ref[:, cols], state)
        )
        residual_ref[:, cols] = residual
        square = square + residual * residual
    inverse = lax.rsqrt(jnp.sum(square, axis=1, keepdims=True) * (1.0 / width) + EPSILON)
    residual = residual_ref[...]
    unit = residual * inverse
    unit_ref[...] = unit
    normed = (unit * gain_ref[...].astype(F32)).astype(BF16)
    logits = mm(normed, router_ref[...], NT)
    names = lax.broadcasted_iota(jnp.int32, (1, experts), 1)
    chosen = [
        jnp.sum(
            jnp.where(names == column([ids_ref[r, k] for r in range(reads)]), logits, 0.0),
            axis=1,
            keepdims=True,
        )
        for k in range(2)
    ]
    first = jax.nn.sigmoid(chosen[0] - chosen[1])
    own = jnp.sum(residual * score_ref[...].astype(F32), axis=1, keepdims=True)
    lane = lax.broadcasted_iota(jnp.int32, (reads, LANES), 1)
    small_ref[...] = jnp.where(lane == 0, inverse, jnp.where(lane == 1, first, own))
    slot = lax.broadcasted_iota(jnp.int32, (slots, 1), 0)
    where = targets(ids_ref, capacity)
    normed = normed.astype(F32)
    out = jnp.zeros((slots, width), F32)
    for r in range(reads):
        out = jnp.where((slot == where[r][0]) | (slot == where[r][1]), normed[r : r + 1], out)
    out_ref[...] = out.astype(BF16)


def route(ids, state, query, lifts, attended, resid, gain, router, score, slots):
    reads, width = query.shape
    vmem = pl.BlockSpec(memory_space=pltpu.VMEM)
    return pl.pallas_call(
        route_body,
        out_shape=(
            jax.ShapeDtypeStruct((slots, width), BF16),
            jax.ShapeDtypeStruct((reads, width), F32),
            jax.ShapeDtypeStruct((reads, LANES), F32),
        ),
        in_specs=[pl.BlockSpec(memory_space=pltpu.SMEM)] + [vmem] * 8,
        out_specs=(vmem,) * 3,
        scratch_shapes=[pltpu.VMEM((reads, width), F32)],
        name="route",
    )(ids, state, query, lifts, attended, resid, gain, router, score)


def slope_body(
    ids_ref, returned_ref, unit_ref, small_ref, gain_ref, router_ref, score_ref, lifted_ref, total_ref,
    slope_ref, payload_ref,
):
    reads, width = unit_ref.shape
    slots = returned_ref.shape[0]
    experts = router_ref.shape[0]
    capacity = slots // experts
    where = targets(ids_ref, capacity)
    spots = [column([where[r][k] for r in range(reads)]) for k in range(2)]
    inverse, first, own = (small_ref[:, i : i + 1] for i in range(3))
    gates = (first, 1.0 - first)
    d_in = jnp.zeros((reads, width), F32)
    scores = [jnp.zeros((reads, 1), F32) for _ in range(2)]
    for slot in range(slots):
        row = returned_ref[slot : slot + 1, :width].astype(F32)
        told = returned_ref[slot : slot + 1, width : width + 1].astype(F32)
        weight = jnp.where(spots[0] == slot, gates[0], 0.0) + jnp.where(spots[1] == slot, gates[1], 0.0)
        d_in = d_in + weight * row
        scores = [s + jnp.where(spot == slot, told, 0.0) for s, spot in zip(scores, spots)]
    own = own + gates[0] * scores[0] + gates[1] * scores[1]
    d_logit = (scores[0] - scores[1]) * gates[0] * gates[1]
    columns = jnp.zeros((reads, width), F32)
    picks = [column([ids_ref[r, k] for r in range(reads)]) for k in range(2)]
    for name in range(experts):
        sign = (picks[0] == name).astype(F32) - (picks[1] == name).astype(F32)
        columns = columns + sign * router_ref[name : name + 1, :].astype(F32)
    d_unit = (d_in + d_logit * columns) * gain_ref[...].astype(F32)
    unit = unit_ref[...]
    mean = jnp.sum(d_unit * unit, axis=1, keepdims=True) * (1.0 / width)
    slope = score_ref[...].astype(F32) + inverse * (d_unit - unit * mean)
    slope_ref[...] = slope
    payload_ref[:, :width] = jnp.concatenate([slope, lifted_ref[...].astype(F32)], axis=0).astype(BF16)
    heads = total_ref.shape[1]
    lane = lax.broadcasted_iota(jnp.int32, (1, LANES), 1)
    total = jnp.concatenate(
        list(parts_of(total_ref[...])) + [jnp.zeros((1, heads), F32)], axis=0
    )
    total = jnp.concatenate([total, jnp.zeros((4, LANES - heads), F32)], axis=1)
    high, middle, rest = parts_of(jnp.sum(own, axis=0, keepdims=True))
    told = jnp.where(lane == 0, high, jnp.where(lane == 1, middle, jnp.where(lane == 2, rest, 0.0)))
    row = lax.broadcasted_iota(jnp.int32, (4, LANES), 0)
    meta = jnp.where(row == 3, told, total)
    payload_ref[:, width:] = jnp.concatenate([meta, jnp.zeros((4, LANES), F32)], axis=0).astype(BF16)


def slope_of(ids, returned, unit, small, gain, router, score, lifted, total):
    reads, width = unit.shape
    vmem = pl.BlockSpec(memory_space=pltpu.VMEM)
    return pl.pallas_call(
        slope_body,
        out_shape=(
            jax.ShapeDtypeStruct((reads, width), F32),
            jax.ShapeDtypeStruct((2 * reads, width + LANES), BF16),
        ),
        in_specs=[pl.BlockSpec(memory_space=pltpu.SMEM)] + [vmem] * 8,
        out_specs=(vmem,) * 2,
        name="slope",
    )(ids, returned, unit, small, gain, router, score, lifted, total)


def share_body(place_ref, meta_ref, out_ref):
    blocks = meta_ref.shape[0]
    ys = place_ref[1]
    own = place_ref[0]
    step = lax.broadcasted_iota(jnp.int32, (blocks, LANES), 0)
    lane = lax.broadcasted_iota(jnp.int32, (blocks, LANES), 1)
    whose = ((own // ys + step // ys) % (blocks // ys)) * ys + (own + step) % ys
    told = jnp.sum(jnp.where(lane < 3, meta_ref[...].astype(F32), 0.0), axis=1, keepdims=True)
    line = jnp.sum(jnp.where(whose == lane, told, 0.0), axis=0, keepdims=True)
    out_ref[...] = jnp.broadcast_to(jnp.sum(line, axis=1, keepdims=True), out_ref.shape)


def share(place, meta, copies):
    return pl.pallas_call(
        share_body,
        out_shape=jax.ShapeDtypeStruct((copies, LANES), F32),
        in_specs=[pl.BlockSpec(memory_space=pltpu.SMEM), pl.BlockSpec(memory_space=pltpu.VMEM)],
        out_specs=pl.BlockSpec(memory_space=pltpu.VMEM),
        name="share",
    )(place, meta)


def scale_body(
    place_ref, order_ref, lengths_ref, sums_ref, keys_ref, values_ref, query_ref, slope_ref,
    loss_ref, query_out, slope_out, keys_out, values_out, *, span, rows, length_weight, score_scale,
):
    count = sums_ref.shape[0]
    reward = sums_ref[...] * (1.0 / rows)
    sub = lax.broadcasted_iota(jnp.int32, (count, LANES), 0)
    lane = lax.broadcasted_iota(jnp.int32, (count, LANES), 1)
    line = jnp.sum(jnp.where(sub == lane, reward, 0.0), axis=0, keepdims=True)
    live = (lax.broadcasted_iota(jnp.int32, (1, LANES), 1) < count).astype(F32)
    share = jnp.zeros((1, LANES), F32)
    for i in range(count):
        share = jnp.where(lane[:1] == i, lengths_ref[i].astype(F32), share)
    share = share * (1.0 / span)
    fitted = jnp.zeros((1, 1), F32)
    slope = jnp.zeros((1, LANES), F32)
    for pair in range(count // 2):
        better, worse = order_ref[2 * pair], order_ref[2 * pair + 1]
        gap = jnp.sum(
            jnp.where(lane[:1] == worse, line, 0.0) - jnp.where(lane[:1] == better, line, 0.0),
            axis=1,
            keepdims=True,
        )
        fitted = fitted + jnp.maximum(gap, 0.0) + jnp.log1p(jnp.exp(-jnp.abs(gap)))
        pull = jax.nn.sigmoid(gap) * (2.0 / count)
        slope = slope + jnp.where(lane[:1] == worse, pull, 0.0) - jnp.where(lane[:1] == better, pull, 0.0)
    def mean(x):
        return jnp.sum(x * live, axis=1, keepdims=True) * (1.0 / count)
    lean = (share - mean(share)) * live
    both = mean((line - mean(line)) * lean)
    loss_ref[...] = jnp.broadcast_to(fitted * (2.0 / count) + length_weight * both * both, loss_ref.shape)
    slope = slope + (2.0 * length_weight / count) * both * (lean - mean(lean))
    factor = jnp.sum(jnp.where(lane[:1] == place_ref[0], slope, 0.0), axis=1, keepdims=True) * score_scale
    query_out[...] = query_ref[...] * factor
    slope_out[...] = slope_ref[...] * factor
    keys_out[...] = (keys_ref[...] * factor).astype(BF16)
    values_out[...] = (values_ref[...] * factor).astype(BF16)


def scale(place, order, lengths, sums, keys, values, query, slope, **sizes):
    smem, vmem = pl.BlockSpec(memory_space=pltpu.SMEM), pl.BlockSpec(memory_space=pltpu.VMEM)
    tokens, width = keys.shape
    reads = query.shape[0]
    return pl.pallas_call(
        functools.partial(scale_body, **sizes),
        out_shape=(
            jax.ShapeDtypeStruct((8, LANES), F32),
            jax.ShapeDtypeStruct((reads, width), F32),
            jax.ShapeDtypeStruct((reads, width), F32),
            jax.ShapeDtypeStruct((tokens, width), BF16),
            jax.ShapeDtypeStruct((tokens, width), BF16),
        ),
        in_specs=[smem] * 3 + [vmem] * 5,
        out_specs=(vmem,) * 5,
        name="scale",
    )(place, order, lengths, sums, keys, values, query, slope)


def prefix_body(bound_ref, terms_ref, out_ref):
    blocks, rows, lanes = out_ref.shape
    near = lax.broadcasted_iota(jnp.int32, (rows, lanes), 0) < bound_ref[0]
    state = jnp.zeros((rows, lanes), jnp.float32)
    for block in range(blocks):
        out_ref[block] = state.astype(jnp.bfloat16)
        tail = terms_ref[block, rows : rows + 8, :].astype(jnp.float32)
        one = jnp.exp(tail[0:1] + tail[1:2] + tail[2:3])
        two = jnp.exp(tail[3:4] + tail[4:5] + tail[5:6])
        state = state * jnp.where(near, one, two) + terms_ref[block, :rows, :].astype(jnp.float32)

def exclusive_states(payload):
    count, rows, lanes = payload.shape
    rows = rows - 8
    size = lanes // 2
    place = lax.axis_index("seq")
    arrived = lax.all_to_all(payload, "seq", 0, 0, tiled=True)
    bound = ((place * rows) // size + 1) * size - place * rows
    vmem = pl.BlockSpec(memory_space=pltpu.VMEM)
    sums = pl.pallas_call(
        prefix_body,
        out_shape=jax.ShapeDtypeStruct((count, rows, lanes), BF16),
        in_specs=[pl.BlockSpec(memory_space=pltpu.SMEM), vmem],
        out_specs=vmem,
        name="state_prefix",
    )(bound.reshape(1), arrived)
    back = lax.all_to_all(sums, "seq", 0, 0, tiled=True)
    return back.reshape(count * rows // size, size, lanes)


def per_device(
    resid_rows,
    query_rows,
    key_rows,
    value_rows,
    log_decay,
    read_pos,
    expert_ids,
    pair_order,
    lengths,
    norm_gain,
    router_weight,
    score_weight,
    gate_weight,
    up_weight,
    down_weight,
):
    seq_count = lax.axis_size("seq")
    exp_count = lax.axis_size("exp")
    seq_index = lax.axis_index("seq")
    exp_index = lax.axis_index("exp")
    zs = seq_count // YS
    token_count = key_rows.shape[1]
    model_width = key_rows.shape[2]
    read_count = query_rows.shape[1]
    expert_count = router_weight.shape[1]
    capacity = max(2, 4 * read_count // exp_count)
    slot_count = expert_count * capacity
    wide = model_width + LANES
    keys, values, query = key_rows[0], value_rows[0], query_rows[0]
    ids = expert_ids[0].astype(jnp.int32)
    gain = norm_gain.reshape(1, model_width)
    score = score_weight.reshape(1, model_width)
    router = router_weight.T
    place = jnp.stack([seq_index, jnp.int32(YS)]).astype(jnp.int32)

    payload, lifted, total, tails, lifts, weights, scores, attended = prepare(
        read_pos[0] - seq_index * token_count, keys, values, query, log_decay[0], seq_count
    )
    state = exclusive_states(payload)
    outgoing, unit, small = route(
        ids, state, query, lifts, attended, resid_rows[0], gain, router, score, slot_count
    )
    arrived = lax.all_to_all(
        outgoing.reshape(expert_count, capacity, model_width), "exp", 0, 0, tiled=True
    ).reshape(slot_count, model_width)
    piece = gather_slots(arrived).reshape(seq_count * slot_count, model_width)

    gate_w = gate_weight[0]
    up_w = up_weight[0]
    down_w = down_weight[0]
    down_score = jnp.sum(down_w.astype(F32) * score.astype(F32), axis=1)
    pre_gate = jnp.dot(piece, gate_w, preferred_element_type=F32)
    pre_up = jnp.dot(piece, up_w, preferred_element_type=F32)
    gate_sigmoid = jax.nn.sigmoid(pre_gate)
    silu = pre_gate * gate_sigmoid
    slot_score = jnp.sum(silu * pre_up * down_score[None, :], axis=1)
    d_pre_gate = (
        down_score[None, :] * pre_up * gate_sigmoid * (1.0 + pre_gate * (1.0 - gate_sigmoid))
    ).astype(BF16)
    d_pre_up = (down_score[None, :] * silu).astype(BF16)
    back = jnp.einsum("sf,df->sd", d_pre_gate, gate_w, preferred_element_type=F32)
    back = back + jnp.einsum("sf,df->sd", d_pre_up, up_w, preferred_element_type=F32)
    score_cols = jnp.pad(slot_score[:, None], ((0, 0), (0, LANES - 1)))
    terms = jnp.concatenate([back, score_cols], axis=1).astype(BF16)
    summed = reduce_slots(terms.reshape(zs, YS, slot_count, wide))
    returned = lax.all_to_all(
        summed.reshape(expert_count, capacity, wide), "exp", 0, 0, tiled=True
    ).reshape(slot_count, wide)

    slope, rows = slope_of(ids, returned, unit, small, gain, router, score, lifted, total)
    rows = gather_small(rows).reshape(seq_count * 2 * read_count, wide)
    meta = rows[:, model_width:].reshape(seq_count, 2 * read_count, LANES)
    sums = share(place, meta[:, 3], exp_count)
    sums = lax.all_to_all(sums.reshape(exp_count, 1, LANES), "exp", 0, 0, tiled=True)
    parts = meta[:, :3].transpose(1, 0, 2)
    grad_keys, grad_values, grad_query = finish(
        place, keys, values, query, slope, rows, parts, state, tails, lifts, weights, scores
    )
    loss, grad_query, grad_resid, grad_keys, grad_values = scale(
        exp_index.reshape(1).astype(jnp.int32),
        pair_order,
        lengths,
        sums.reshape(exp_count, LANES),
        grad_keys,
        grad_values,
        grad_query,
        slope,
        span=token_count * seq_count,
        rows=read_count * seq_count,
        length_weight=LENGTH_WEIGHT,
        score_scale=SCORE_SCALE,
    )
    return (loss[0, 0], grad_query[None], grad_resid[None], grad_keys[None], grad_values[None])


def solution(mesh):
    in_specs = (
        P("exp", "seq", None),
        P("exp", "seq", None),
        P("exp", "seq", None),
        P("exp", "seq", None),
        P("exp", None, "seq"),
        P("exp", "seq"),
        P("exp", "seq", None),
        P(),
        P(),
        P(),
        P(),
        P(),
        P("exp", None, "seq"),
        P("exp", None, "seq"),
        P("exp", "seq", None),
    )
    out_specs = (
        P(),
        P("exp", "seq", None),
        P("exp", "seq", None),
        P("exp", "seq", None),
        P("exp", "seq", None),
    )
    return jax.shard_map(
        per_device, mesh=mesh, in_specs=in_specs, out_specs=out_specs, check_vma=False
    )
```

```python
import functools

import jax
import jax.numpy as jnp
import numpy as np
from jax import lax
from jax.experimental import pallas as pl
from jax.experimental.pallas import tpu as pltpu
from jax.sharding import PartitionSpec as P

EPSILON = 1e-06
LENGTH_WEIGHT = 4.0
SCORE_SCALE = 256.0
YS = 4
LANES = 128


def receive(value, dz, dy):
    zs = lax.axis_size("seq") // YS
    pairs = [
        (((z + dz) % zs) * YS + (y + dy) % YS, z * YS + y) for z in range(zs) for y in range(YS)
    ]
    return lax.ppermute(value, "seq", pairs)


def split_cols(value):
    half = -(-value.shape[-1] // (2 * LANES)) * LANES
    return value[..., :half], value[..., half:]


def shifted(axis):
    if axis == "z":
        return lambda value, step: receive(value, step, 0)
    return lambda value, step: receive(value, 0, step)


def direct_gather(own, axis, count):
    get = shifted(axis)
    return [own] + [get(own, step if step <= count // 2 else step - count) for step in range(1, count)]


def ring_gather(own, axis, count, halves):
    get = shifted(axis)
    blocks = [None] * count
    blocks[0] = own
    ahead = behind = own
    for lap in range(1, count // 2):
        ahead, behind = get(ahead, 1), get(behind, -1)
        blocks[lap], blocks[count - lap] = ahead, behind
    if halves:
        first, _ = split_cols(ahead)
        _, second = split_cols(behind)
        blocks[count // 2] = jnp.concatenate([get(first, 1), get(second, -1)], axis=-1)
    else:
        blocks[count // 2] = get(ahead, 1)
    return blocks


def add_rounded(left, right):
    return (left.astype(jnp.float32) + right.astype(jnp.float32)).astype(jnp.bfloat16)


def direct_reduce(blocks, axis):
    get = shifted(axis)
    count = len(blocks)
    total = blocks[0].astype(jnp.float32)
    for step in range(1, count):
        total = total + get(
            blocks[step], -step if step <= count // 2 else count - step
        ).astype(jnp.float32)
    return total.astype(jnp.bfloat16)


def ring_reduce(blocks, axis, halves):
    get = shifted(axis)
    count = len(blocks)
    middle = count // 2
    blocks = list(blocks)
    if halves:
        first, second = split_cols(blocks[middle])
        first, second = get(first, -1), get(second, 1)
        half = first.shape[-1]
        up, down = blocks[middle - 1], blocks[middle + 1]
        blocks[middle - 1] = jnp.concatenate(
            [add_rounded(up[..., :half], first), up[..., half:]], axis=-1
        )
        blocks[middle + 1] = jnp.concatenate(
            [down[..., :half], add_rounded(down[..., half:], second)], axis=-1
        )
    else:
        blocks[middle - 1] = add_rounded(blocks[middle - 1], get(blocks[middle], -1))
    first, second = blocks[middle - 1], blocks[middle + 1]
    for lap in range(middle - 1, 0, -1):
        first, second = get(first, -1), get(second, 1)
        if lap > 1:
            first = add_rounded(blocks[lap - 1], first)
            second = add_rounded(blocks[count - lap + 1], second)
    total = (
        blocks[0].astype(jnp.float32) + first.astype(jnp.float32) + second.astype(jnp.float32)
    )
    return total.astype(jnp.bfloat16)


def cut_of(width):
    return -(-width // (2 * LANES)) * LANES


def along_z(blocks):
    zs = blocks.shape[0]
    groups = [[z * YS + y for z in range(zs)] for y in range(YS)]
    return lax.all_to_all(blocks, "seq", 0, 0, axis_index_groups=groups, tiled=True)


def turned(blocks, start):
    return lax.dynamic_slice_in_dim(jnp.concatenate([blocks, blocks]), start, blocks.shape[0], 0)


def gather_slots(rows):
    zs = lax.axis_size("seq") // YS
    own_z = lax.axis_index("seq") // YS
    cut = cut_of(rows.shape[-1])
    left = jnp.stack(direct_gather(rows[:, :cut], "y", YS))
    right = rows[:, cut:]
    right = along_z(jnp.broadcast_to(right, (zs,) + right.shape))
    left, (right,) = ring_with(left, "z", zs, right, {2: lambda blocks: turned(blocks, own_z)})
    left = jnp.stack(left)
    right = jnp.stack(ring_gather(right, "y", YS, True), axis=1)
    return jnp.concatenate([left, right], axis=-1)


def reduce_slots(terms):
    zs = terms.shape[0]
    own_z = lax.axis_index("seq") // YS
    cut = cut_of(terms.shape[-1])
    left = ring_reduce([terms[dz, :, :, :cut] for dz in range(zs)], "z", False)
    right = ring_reduce([terms[:, dy, :, cut:] for dy in range(YS)], "y", True)
    right = along_z(turned(right, (zs - own_z) % zs))
    left = direct_reduce([left[dy] for dy in range(YS)], "y")
    right = jnp.sum(right.astype(jnp.float32), axis=0).astype(jnp.bfloat16)
    return jnp.concatenate([left, right], axis=-1)


def ring_with(own, axis, count, operand, work):
    get = shifted(axis)
    blocks = [None] * count
    blocks[0] = own
    ahead = behind = own
    done = []
    for lap in range(1, count // 2):
        if lap in work:
            ahead, behind, operand = lax.optimization_barrier((ahead, behind, operand))
        ahead, behind = get(ahead, 1), get(behind, -1)
        blocks[lap], blocks[count - lap] = ahead, behind
        if lap in work:
            ahead, behind, piece = lax.optimization_barrier((ahead, behind, work[lap](operand)))
            done.append(piece)
    blocks[count // 2] = get(ahead, 1)
    return blocks, done


F32 = jnp.float32
BF16 = jnp.bfloat16

NT = (((1,), (1,)), ((), ()))
TN = (((0,), (0,)), ((), ()))
NN = (((1,), (0,)), ((), ()))


def mm(left, right, dims=NN):
    return lax.dot_general(left, right, dims, preferred_element_type=F32)


def parts_of(value):
    high = value.astype(BF16).astype(F32)
    middle = (value - high).astype(BF16).astype(F32)
    return high, middle, (value - high - middle).astype(BF16).astype(F32)


def by_half(left, right, low):
    return jnp.where(low, left, right)


def both_rows(rows, low):
    zero = jnp.zeros_like(rows)
    return jnp.concatenate([jnp.where(low, rows, zero), jnp.where(low, zero, rows)], axis=0)


def prepare_body(
    places_ref, keys_ref, values_ref, query_ref, decay_ref,
    payload_ref, lifted_ref, total_ref, tails_ref, lifts_ref, weights_ref, scores_ref, attended_ref, spread_ref,
):
    tokens, width = keys_ref.shape
    reads = query_ref.shape[0]
    heads = decay_ref.shape[0]
    pairs = heads // 2
    size = width // heads
    blocks, _, _ = payload_ref.shape
    rows = pairs * size // blocks
    decay = decay_ref[...]
    t0 = lax.broadcasted_iota(jnp.int32, (tokens, tokens), 0)
    t1 = lax.broadcasted_iota(jnp.int32, (tokens, tokens), 1)
    lower = (t1 <= t0).astype(F32)
    upper = (t0 <= t1).astype(F32)
    cum = sum(mm(part.astype(BF16), upper.astype(BF16)) for part in parts_of(decay))
    cum_t = sum(mm(lower.astype(BF16), part.astype(BF16), NT) for part in parts_of(decay))
    spread_ref[...] = cum_t
    total_ref[...] = cum_t[tokens - 1 : tokens]
    tail = jnp.exp(cum_t[tokens - 1 : tokens] - cum_t)
    tails_ref[...] = tail
    total = cum[:, tokens - 1 : tokens]
    at_read = jnp.concatenate([spread_ref[pl.ds(places_ref[r], 1), :] for r in range(reads)], axis=0)
    lift = jnp.exp(at_read)
    lifts_ref[...] = lift
    lane = lax.broadcasted_iota(jnp.int32, (1, LANES), 1)
    low = lane < size
    spot = lax.broadcasted_iota(jnp.int32, (reads, tokens), 1)
    row = lax.broadcasted_iota(jnp.int32, (reads, tokens), 0)
    place = jnp.zeros((reads, tokens), jnp.int32)
    for r in range(reads):
        place = jnp.where(row == r, places_ref[r], place)
    allowed = spot <= place
    lanes_total = []
    for p in range(pairs):
        cols = slice(p * LANES, (p + 1) * LANES)
        one, two = 2 * p, 2 * p + 1
        key, value, query = keys_ref[:, cols], values_ref[:, cols], query_ref[:, cols]
        fade = by_half(tail[:, one : one + 1], tail[:, two : two + 1], low)
        state = mm((key.astype(F32) * fade).astype(BF16), value, TN)
        state = by_half(state[:size], state[size:], low).astype(BF16)
        for chunk in range(size // 16):
            where = p * (size // 16) + chunk
            block, offset = where // (rows // 16), where % (rows // 16)
            payload_ref[block, offset * 16 : offset * 16 + 16, :] = state[chunk * 16 : chunk * 16 + 16]
        lanes_total.append(by_half(total[one : one + 1], total[two : two + 1], low))
        raised = by_half(lift[:, one : one + 1], lift[:, two : two + 1], low)
        lifted_ref[:, cols] = (query.astype(F32) * raised).astype(BF16)
        weight = [
            jnp.exp(jnp.where(allowed, at_read[:, h : h + 1] - cum[h : h + 1, :], -1e30))
            for h in (one, two)
        ]
        weight = jnp.concatenate(weight, axis=0)
        weights_ref[p] = weight
        score = weight * mm(both_rows(query, low), key, NT) * (1.0 / size)
        scores_ref[p] = score
        near = mm(score.astype(BF16), value)
        attended_ref[:, cols] = by_half(near[:reads], near[reads:], low)
    for block in range(blocks):
        first = block * rows // size
        last = (block * rows + rows - 1) // size
        meta = list(parts_of(lanes_total[first])) + list(parts_of(lanes_total[last]))
        meta = jnp.concatenate(meta + [jnp.zeros((2, LANES), F32)], axis=0)
        payload_ref[block, rows : rows + 8, :] = meta.astype(BF16)


def prepare(places, keys, values, query, decay, blocks):
    tokens, width = keys.shape
    reads = query.shape[0]
    heads = decay.shape[0]
    pairs = heads // 2
    rows = pairs * (width // heads) // blocks
    vmem = pl.BlockSpec(memory_space=pltpu.VMEM)
    return pl.pallas_call(
        prepare_body,
        out_shape=(
            jax.ShapeDtypeStruct((blocks, rows + 8, LANES), BF16),
            jax.ShapeDtypeStruct((reads, width), BF16),
            jax.ShapeDtypeStruct((1, heads), F32),
            jax.ShapeDtypeStruct((tokens, heads), F32),
            jax.ShapeDtypeStruct((reads, heads), F32),
            jax.ShapeDtypeStruct((pairs, 2 * reads, tokens), F32),
            jax.ShapeDtypeStruct((pairs, 2 * reads, tokens), F32),
            jax.ShapeDtypeStruct((reads, width), F32),
        ),
        in_specs=[pl.BlockSpec(memory_space=pltpu.SMEM)] + [vmem] * 4,
        out_specs=(vmem,) * 8,
        scratch_shapes=[pltpu.VMEM((tokens, heads), F32)],
        name="prepare",
    )(places, keys, values, query, decay)


def near_body(
    keys_ref, values_ref, query_ref, slope_ref, state_ref, lifts_ref, weights_ref, scores_ref,
    keys_out, values_out, query_out, *, start,
):
    reads = query_ref.shape[0]
    pairs = keys_out.shape[1] // LANES
    size = keys_ref.shape[1] // lifts_ref.shape[1]
    low = lax.broadcasted_iota(jnp.int32, (1, LANES), 1) < size
    lift = lifts_ref[...]
    for q in range(pairs):
        p = start + q
        cols, outs = slice(p * LANES, (p + 1) * LANES), slice(q * LANES, (q + 1) * LANES)
        one, two = 2 * p, 2 * p + 1
        key, value, query = keys_ref[:, cols], values_ref[:, cols], query_ref[:, cols]
        slope = slope_ref[:, cols].astype(BF16)
        slopes = both_rows(slope, low)
        near = (weights_ref[p] * mm(slopes, value, NT) * (1.0 / size)).astype(BF16)
        keys_out[:, outs] = mm(near, both_rows(query, low), TN)
        values_out[:, outs] = mm(scores_ref[p].astype(BF16), slopes, TN)
        state = state_ref[p]
        zero = jnp.zeros_like(state)
        state = jnp.concatenate([jnp.where(low, state, zero), jnp.where(low, zero, state)], axis=0)
        raised = by_half(lift[:, one : one + 1], lift[:, two : two + 1], low) * (1.0 / size)
        own = mm(near, key)
        query_out[:, outs] = by_half(own[:reads], own[reads:], low) + raised * mm(slope, state, NT)


def near_terms(start, pairs, keys, values, query, slope, state, lifts, weights, scores):
    tokens, reads = keys.shape[0], query.shape[0]
    vmem = pl.BlockSpec(memory_space=pltpu.VMEM)
    return pl.pallas_call(
        functools.partial(near_body, start=start),
        out_shape=(
            jax.ShapeDtypeStruct((tokens, pairs * LANES), F32),
            jax.ShapeDtypeStruct((tokens, pairs * LANES), F32),
            jax.ShapeDtypeStruct((reads, pairs * LANES), F32),
        ),
        in_specs=[vmem] * 8,
        out_specs=(vmem,) * 3,
        name="near",
    )(keys, values, query, slope, state, lifts, weights, scores)


def far_body(place_ref, keys_ref, values_ref, far_ref, tails_ref, keys_out, values_out, *, reads):
    tokens, width = keys_ref.shape
    heads = tails_ref.shape[1]
    pairs = heads // 2
    size = width // heads
    low = lax.broadcasted_iota(jnp.int32, (1, LANES), 1) < size
    r0 = lax.broadcasted_iota(jnp.int32, (LANES, LANES), 0) < size
    r1 = lax.broadcasted_iota(jnp.int32, (LANES, LANES), 1) < size
    same = r0 == r1
    tail = tails_ref[...]
    own, ys = place_ref[0], place_ref[1]
    count = far_ref.shape[0]
    blocks = count // (2 * reads)

    def whose(step):
        return ((own // ys + step // ys) % (blocks // ys)) * ys + (own + step) % ys

    row = lax.broadcasted_iota(jnp.int32, (count, count), 0)
    col = lax.broadcasted_iota(jnp.int32, (count, count), 1)
    other = whose(col // (2 * reads))
    mine = whose(row // (2 * reads))
    between = ((other > own) & (other < mine) & (col % (2 * reads) < 3)).astype(BF16)
    reach = jnp.exp(mm(between, far_ref[:, width : width + LANES]))
    later = (mine[:, :1] > own) & (row[:, :1] % (2 * reads) < reads)
    reach = jnp.where(later, reach, 0.0) * (1.0 / size)
    for p in range(pairs):
        cols = slice(p * LANES, (p + 1) * LANES)
        one, two = 2 * p, 2 * p + 1
        far = by_half(reach[:, one : one + 1], reach[:, two : two + 1], low)
        rows = far_ref[:, cols]
        far = (pltpu.roll(rows.astype(F32), count - reads, 0) * far).astype(BF16)
        suffix = jnp.where(same, mm(far, rows, TN), 0.0).astype(BF16)
        fade = by_half(tail[:, one : one + 1], tail[:, two : two + 1], low)
        keys_out[:, cols] = fade * mm(values_ref[:, cols], suffix, NT)
        values_out[:, cols] = fade * mm(keys_ref[:, cols], suffix)


def far_terms(place, keys, values, far, tails, reads):
    tokens, width = keys.shape
    vmem = pl.BlockSpec(memory_space=pltpu.VMEM)
    return pl.pallas_call(
        functools.partial(far_body, reads=reads),
        out_shape=(jax.ShapeDtypeStruct((tokens, width), F32),) * 2,
        in_specs=[pl.BlockSpec(memory_space=pltpu.SMEM)] + [vmem] * 4,
        out_specs=(vmem,) * 2,
        name="far",
    )(place, keys, values, far, tails)


def targets(ids_ref, capacity):
    reads = ids_ref.shape[0]
    out = []
    for r in range(reads):
        mine = []
        for k in range(2):
            name = ids_ref[r, k]
            slot = name * capacity
            for q in range(r):
                slot = slot + (ids_ref[q, 0] == name).astype(jnp.int32)
                slot = slot + (ids_ref[q, 1] == name).astype(jnp.int32)
            mine.append(slot)
        out.append(mine)
    return out


def column(scalars):
    rows = lax.broadcasted_iota(jnp.int32, (len(scalars), 1), 0)
    out = jnp.zeros((len(scalars), 1), jnp.int32)
    for r, scalar in enumerate(scalars):
        out = jnp.where(rows == r, scalar, out)
    return out


def route_body(
    ids_ref, state_ref, query_ref, lifts_ref, attended_ref, resid_ref, gain_ref, router_ref, score_ref,
    out_ref, unit_ref, small_ref, residual_ref,
):
    reads, width = query_ref.shape
    heads = lifts_ref.shape[1]
    pairs = heads // 2
    size = width // heads
    slots = out_ref.shape[0]
    experts = router_ref.shape[0]
    capacity = slots // experts
    low = lax.broadcasted_iota(jnp.int32, (1, LANES), 1) < size
    lift = lifts_ref[...]
    square = jnp.zeros((reads, LANES), F32)
    for p in range(pairs):
        cols = slice(p * LANES, (p + 1) * LANES)
        one, two = 2 * p, 2 * p + 1
        state = state_ref[p]
        zero = jnp.zeros_like(state)
        state = jnp.concatenate([jnp.where(low, state, zero), jnp.where(low, zero, state)], axis=0)
        raised = by_half(lift[:, one : one + 1], lift[:, two : two + 1], low) * (1.0 / size)
        residual = (
            resid_ref[:, cols].astype(F32) + attended_ref[:, cols] + raised * mm(query_ref[:, cols], state)
        )
        residual_ref[:, cols] = residual
        square = square + residual * residual
    inverse = lax.rsqrt(jnp.sum(square, axis=1, keepdims=True) * (1.0 / width) + EPSILON)
    residual = residual_ref[...]
    unit = residual * inverse
    unit_ref[...] = unit
    normed = (unit * gain_ref[...].astype(F32)).astype(BF16)
    logits = mm(normed, router_ref[...], NT)
    names = lax.broadcasted_iota(jnp.int32, (1, experts), 1)
    chosen = [
        jnp.sum(
            jnp.where(names == column([ids_ref[r, k] for r in range(reads)]), logits, 0.0),
            axis=1,
            keepdims=True,
        )
        for k in range(2)
    ]
    first = jax.nn.sigmoid(chosen[0] - chosen[1])
    own = jnp.sum(residual * score_ref[...].astype(F32), axis=1, keepdims=True)
    lane = lax.broadcasted_iota(jnp.int32, (reads, LANES), 1)
    small_ref[...] = jnp.where(lane == 0, inverse, jnp.where(lane == 1, first, own))
    slot = lax.broadcasted_iota(jnp.int32, (slots, 1), 0)
    where = targets(ids_ref, capacity)
    normed = normed.astype(F32)
    out = jnp.zeros((slots, width), F32)
    for r in range(reads):
        out = jnp.where((slot == where[r][0]) | (slot == where[r][1]), normed[r : r + 1], out)
    out_ref[...] = out.astype(BF16)


def route(ids, state, query, lifts, attended, resid, gain, router, score, slots):
    reads, width = query.shape
    vmem = pl.BlockSpec(memory_space=pltpu.VMEM)
    return pl.pallas_call(
        route_body,
        out_shape=(
            jax.ShapeDtypeStruct((slots, width), BF16),
            jax.ShapeDtypeStruct((reads, width), F32),
            jax.ShapeDtypeStruct((reads, LANES), F32),
        ),
        in_specs=[pl.BlockSpec(memory_space=pltpu.SMEM)] + [vmem] * 8,
        out_specs=(vmem,) * 3,
        scratch_shapes=[pltpu.VMEM((reads, width), F32)],
        name="route",
    )(ids, state, query, lifts, attended, resid, gain, router, score)


def slope_body(
    ids_ref, returned_ref, unit_ref, small_ref, gain_ref, router_ref, score_ref, lifted_ref, total_ref,
    slope_ref, payload_ref,
):
    reads, width = unit_ref.shape
    slots = returned_ref.shape[0]
    experts = router_ref.shape[0]
    capacity = slots // experts
    where = targets(ids_ref, capacity)
    spots = [column([where[r][k] for r in range(reads)]) for k in range(2)]
    inverse, first, own = (small_ref[:, i : i + 1] for i in range(3))
    gates = (first, 1.0 - first)
    d_in = jnp.zeros((reads, width), F32)
    scores = [jnp.zeros((reads, 1), F32) for _ in range(2)]
    for slot in range(slots):
        row = returned_ref[slot : slot + 1, :width].astype(F32)
        told = returned_ref[slot : slot + 1, width : width + 1].astype(F32)
        weight = jnp.where(spots[0] == slot, gates[0], 0.0) + jnp.where(spots[1] == slot, gates[1], 0.0)
        d_in = d_in + weight * row
        scores = [s + jnp.where(spot == slot, told, 0.0) for s, spot in zip(scores, spots)]
    own = own + gates[0] * scores[0] + gates[1] * scores[1]
    d_logit = (scores[0] - scores[1]) * gates[0] * gates[1]
    columns = jnp.zeros((reads, width), F32)
    picks = [column([ids_ref[r, k] for r in range(reads)]) for k in range(2)]
    for name in range(experts):
        sign = (picks[0] == name).astype(F32) - (picks[1] == name).astype(F32)
        columns = columns + sign * router_ref[name : name + 1, :].astype(F32)
    d_unit = (d_in + d_logit * columns) * gain_ref[...].astype(F32)
    unit = unit_ref[...]
    mean = jnp.sum(d_unit * unit, axis=1, keepdims=True) * (1.0 / width)
    slope = score_ref[...].astype(F32) + inverse * (d_unit - unit * mean)
    slope_ref[...] = slope
    payload_ref[:, :width] = jnp.concatenate([slope, lifted_ref[...].astype(F32)], axis=0).astype(BF16)
    heads = total_ref.shape[1]
    lane = lax.broadcasted_iota(jnp.int32, (1, LANES), 1)
    total = jnp.concatenate(
        list(parts_of(total_ref[...])) + [jnp.zeros((1, heads), F32)], axis=0
    )
    total = jnp.concatenate([total, jnp.zeros((4, LANES - heads), F32)], axis=1)
    high, middle, rest = parts_of(jnp.sum(own, axis=0, keepdims=True))
    told = jnp.where(lane == 0, high, jnp.where(lane == 1, middle, jnp.where(lane == 2, rest, 0.0)))
    row = lax.broadcasted_iota(jnp.int32, (4, LANES), 0)
    meta = jnp.where(row == 3, told, total)
    payload_ref[:, width:] = jnp.concatenate([meta, jnp.zeros((4, LANES), F32)], axis=0).astype(BF16)


def slope_of(ids, returned, unit, small, gain, router, score, lifted, total):
    reads, width = unit.shape
    vmem = pl.BlockSpec(memory_space=pltpu.VMEM)
    return pl.pallas_call(
        slope_body,
        out_shape=(
            jax.ShapeDtypeStruct((reads, width), F32),
            jax.ShapeDtypeStruct((2 * reads, width + LANES), BF16),
        ),
        in_specs=[pl.BlockSpec(memory_space=pltpu.SMEM)] + [vmem] * 8,
        out_specs=(vmem,) * 2,
        name="slope",
    )(ids, returned, unit, small, gain, router, score, lifted, total)


def share_body(place_ref, meta_ref, out_ref, *, reads):
    count = meta_ref.shape[0]
    blocks = count // (2 * reads)
    own, ys = place_ref[0], place_ref[1]
    row = lax.broadcasted_iota(jnp.int32, (count, LANES), 0)
    lane = lax.broadcasted_iota(jnp.int32, (count, LANES), 1)
    step = row // (2 * reads)
    whose = ((own // ys + step // ys) % (blocks // ys)) * ys + (own + step) % ys
    live = (lane < 3) & (row % (2 * reads) == 3)
    told = jnp.sum(jnp.where(live, meta_ref[...].astype(F32), 0.0), axis=1, keepdims=True)
    line = jnp.sum(jnp.where(whose == lane, told, 0.0), axis=0, keepdims=True)
    out_ref[...] = jnp.broadcast_to(jnp.sum(line, axis=1, keepdims=True), out_ref.shape)


def share(place, rows, copies, reads):
    count, wide = rows.shape
    return pl.pallas_call(
        functools.partial(share_body, reads=reads),
        out_shape=jax.ShapeDtypeStruct((copies, LANES), F32),
        grid=(1,),
        in_specs=[
            pl.BlockSpec(memory_space=pltpu.SMEM),
            pl.BlockSpec((count, LANES), lambda i: (0, wide // LANES - 1)),
        ],
        out_specs=pl.BlockSpec((copies, LANES), lambda i: (0, 0)),
        name="share",
    )(place, rows)


def scale_body(
    place_ref, order_ref, lengths_ref, sums_ref, keys_ref, values_ref, slope_ref, *refs,
    span, rows, length_weight, score_scale,
):
    near_refs = refs[:-5]
    loss_ref, query_out, slope_out, keys_out, values_out = refs[-5:]
    count = sums_ref.shape[0]
    reward = sums_ref[...] * (1.0 / rows)
    sub = lax.broadcasted_iota(jnp.int32, (count, LANES), 0)
    lane = lax.broadcasted_iota(jnp.int32, (count, LANES), 1)
    line = jnp.sum(jnp.where(sub == lane, reward, 0.0), axis=0, keepdims=True)
    live = (lax.broadcasted_iota(jnp.int32, (1, LANES), 1) < count).astype(F32)
    share = jnp.zeros((1, LANES), F32)
    for i in range(count):
        share = jnp.where(lane[:1] == i, lengths_ref[i].astype(F32), share)
    share = share * (1.0 / span)
    fitted = jnp.zeros((1, 1), F32)
    slope = jnp.zeros((1, LANES), F32)
    for pair in range(count // 2):
        better, worse = order_ref[2 * pair], order_ref[2 * pair + 1]
        gap = jnp.sum(
            jnp.where(lane[:1] == worse, line, 0.0) - jnp.where(lane[:1] == better, line, 0.0),
            axis=1,
            keepdims=True,
        )
        fitted = fitted + jnp.maximum(gap, 0.0) + jnp.log1p(jnp.exp(-jnp.abs(gap)))
        pull = jax.nn.sigmoid(gap) * (2.0 / count)
        slope = slope + jnp.where(lane[:1] == worse, pull, 0.0) - jnp.where(lane[:1] == better, pull, 0.0)
    def mean(x):
        return jnp.sum(x * live, axis=1, keepdims=True) * (1.0 / count)
    lean = (share - mean(share)) * live
    both = mean((line - mean(line)) * lean)
    loss_ref[...] = jnp.broadcast_to(fitted * (2.0 / count) + length_weight * both * both, loss_ref.shape)
    slope = slope + (2.0 * length_weight / count) * both * (lean - mean(lean))
    factor = jnp.sum(jnp.where(lane[:1] == place_ref[0], slope, 0.0), axis=1, keepdims=True) * score_scale
    slope_out[...] = slope_ref[...] * factor
    at = 0
    for i in range(0, len(near_refs), 3):
        near_keys, near_values, near_query = near_refs[i : i + 3]
        cols = slice(at, at + near_keys.shape[1])
        at = at + near_keys.shape[1]
        keys_out[:, cols] = ((keys_ref[:, cols] + near_keys[...]) * factor).astype(BF16)
        values_out[:, cols] = ((values_ref[:, cols] + near_values[...]) * factor).astype(BF16)
        query_out[:, cols] = near_query[...] * factor


def scale(place, order, lengths, sums, keys, values, slope, near, **sizes):
    smem, vmem = pl.BlockSpec(memory_space=pltpu.SMEM), pl.BlockSpec(memory_space=pltpu.VMEM)
    tokens, width = keys.shape
    reads = slope.shape[0]
    return pl.pallas_call(
        functools.partial(scale_body, **sizes),
        out_shape=(
            jax.ShapeDtypeStruct((1, 1), F32),
            jax.ShapeDtypeStruct((reads, width), F32),
            jax.ShapeDtypeStruct((reads, width), F32),
            jax.ShapeDtypeStruct((tokens, width), BF16),
            jax.ShapeDtypeStruct((tokens, width), BF16),
        ),
        in_specs=[smem] * 3 + [vmem] * (4 + len(near)),
        out_specs=(vmem,) * 5,
        name="scale",
    )(place, order, lengths, sums, keys, values, slope, *near)


def prefix_body(bound_ref, terms_ref, out_ref):
    blocks, rows, lanes = out_ref.shape
    near = lax.broadcasted_iota(jnp.int32, (rows, lanes), 0) < bound_ref[0]
    state = jnp.zeros((rows, lanes), jnp.float32)
    for block in range(blocks):
        out_ref[block] = state.astype(jnp.bfloat16)
        tail = terms_ref[block, rows : rows + 8, :].astype(jnp.float32)
        one = jnp.exp(tail[0:1] + tail[1:2] + tail[2:3])
        two = jnp.exp(tail[3:4] + tail[4:5] + tail[5:6])
        state = state * jnp.where(near, one, two) + terms_ref[block, :rows, :].astype(jnp.float32)

def exclusive_states(payload):
    count, rows, lanes = payload.shape
    rows = rows - 8
    size = lanes // 2
    place = lax.axis_index("seq")
    arrived = lax.all_to_all(payload, "seq", 0, 0, tiled=True)
    bound = ((place * rows) // size + 1) * size - place * rows
    vmem = pl.BlockSpec(memory_space=pltpu.VMEM)
    sums = pl.pallas_call(
        prefix_body,
        out_shape=jax.ShapeDtypeStruct((count, rows, lanes), BF16),
        in_specs=[pl.BlockSpec(memory_space=pltpu.SMEM), vmem],
        out_specs=vmem,
        name="state_prefix",
    )(bound.reshape(1), arrived)
    back = lax.all_to_all(sums, "seq", 0, 0, tiled=True)
    return back.reshape(count * rows // size, size, lanes)


def per_device(
    resid_rows,
    query_rows,
    key_rows,
    value_rows,
    log_decay,
    read_pos,
    expert_ids,
    pair_order,
    lengths,
    norm_gain,
    router_weight,
    score_weight,
    gate_weight,
    up_weight,
    down_weight,
):
    seq_count = lax.axis_size("seq")
    exp_count = lax.axis_size("exp")
    seq_index = lax.axis_index("seq")
    exp_index = lax.axis_index("exp")
    zs = seq_count // YS
    token_count = key_rows.shape[1]
    model_width = key_rows.shape[2]
    read_count = query_rows.shape[1]
    expert_count = router_weight.shape[1]
    capacity = max(2, 4 * read_count // exp_count)
    slot_count = expert_count * capacity
    wide = model_width + LANES
    keys, values, query = key_rows[0], value_rows[0], query_rows[0]
    ids = expert_ids[0].astype(jnp.int32)
    gain = norm_gain.reshape(1, model_width)
    score = score_weight.reshape(1, model_width)
    router = router_weight.T
    place = jnp.stack([seq_index, jnp.int32(YS)]).astype(jnp.int32)

    payload, lifted, total, tails, lifts, weights, scores, attended = prepare(
        read_pos[0] - seq_index * token_count, keys, values, query, log_decay[0], seq_count
    )
    state = exclusive_states(payload)
    outgoing, unit, small = route(
        ids, state, query, lifts, attended, resid_rows[0], gain, router, score, slot_count
    )
    arrived = lax.all_to_all(
        outgoing.reshape(expert_count, capacity, model_width), "exp", 0, 0, tiled=True
    ).reshape(slot_count, model_width)
    piece = gather_slots(arrived).reshape(seq_count * slot_count, model_width)

    gate_w = gate_weight[0]
    up_w = up_weight[0]
    down_w = down_weight[0]
    down_score = jnp.sum(down_w.astype(F32) * score.astype(F32), axis=1)
    pre_gate = jnp.dot(piece, gate_w, preferred_element_type=F32)
    pre_up = jnp.dot(piece, up_w, preferred_element_type=F32)
    gate_sigmoid = jax.nn.sigmoid(pre_gate)
    silu = pre_gate * gate_sigmoid
    slot_score = jnp.sum(silu * pre_up * down_score[None, :], axis=1)
    d_pre_gate = (
        down_score[None, :] * pre_up * gate_sigmoid * (1.0 + pre_gate * (1.0 - gate_sigmoid))
    ).astype(BF16)
    d_pre_up = (down_score[None, :] * silu).astype(BF16)
    back = jnp.einsum("sf,df->sd", d_pre_gate, gate_w, preferred_element_type=F32)
    back = back + jnp.einsum("sf,df->sd", d_pre_up, up_w, preferred_element_type=F32)
    score_cols = jnp.pad(slot_score[:, None], ((0, 0), (0, LANES - 1)))
    terms = jnp.concatenate([back, score_cols], axis=1).astype(BF16)
    summed = reduce_slots(terms.reshape(zs, YS, slot_count, wide))
    returned = lax.all_to_all(
        summed.reshape(expert_count, capacity, wide), "exp", 0, 0, tiled=True
    ).reshape(slot_count, wide)

    slope, rows = slope_of(ids, returned, unit, small, gain, router, score, lifted, total)
    block = jnp.stack(direct_gather(rows, "y", YS))
    pairs = model_width // LANES
    half = pairs // 2

    def near_half(start):
        return lambda held: near_terms(
            start, half, keys, values, held, slope, state, lifts, weights, scores
        )

    rows, near = ring_with(block, "z", zs, query, {1: near_half(0), 2: near_half(half)})
    rows = jnp.stack(rows).reshape(seq_count * 2 * read_count, wide)
    sums = share(place, rows, exp_count, read_count)
    sums = lax.all_to_all(sums.reshape(exp_count, 1, LANES), "exp", 0, 0, tiled=True)
    grad_keys, grad_values = far_terms(place, keys, values, rows, tails, read_count)
    loss, grad_query, grad_resid, grad_keys, grad_values = scale(
        exp_index.reshape(1).astype(jnp.int32),
        pair_order,
        lengths,
        sums.reshape(exp_count, LANES),
        grad_keys,
        grad_values,
        slope,
        near[0] + near[1],
        span=token_count * seq_count,
        rows=read_count * seq_count,
        length_weight=LENGTH_WEIGHT,
        score_scale=SCORE_SCALE,
    )
    return (loss.reshape(()), grad_query[None], grad_resid[None], grad_keys[None], grad_values[None])


def solution(mesh):
    in_specs = (
        P("exp", "seq", None),
        P("exp", "seq", None),
        P("exp", "seq", None),
        P("exp", "seq", None),
        P("exp", None, "seq"),
        P("exp", "seq"),
        P("exp", "seq", None),
        P(),
        P(),
        P(),
        P(),
        P(),
        P("exp", None, "seq"),
        P("exp", None, "seq"),
        P("exp", "seq", None),
    )
    out_specs = (
        P(),
        P("exp", "seq", None),
        P("exp", "seq", None),
        P("exp", "seq", None),
        P("exp", "seq", None),
    )
    return jax.shard_map(
        per_device, mesh=mesh, in_specs=in_specs, out_specs=out_specs, check_vma=False
    )
```

```python
import functools

import jax
import jax.numpy as jnp
import numpy as np
from jax import lax
from jax.experimental import pallas as pl
from jax.experimental.pallas import tpu as pltpu
from jax.sharding import PartitionSpec as P

EPSILON = 1e-06
LENGTH_WEIGHT = 4.0
SCORE_SCALE = 256.0
YS = 4
LANES = 128


def receive(value, dz, dy):
    zs = lax.axis_size("seq") // YS
    pairs = [
        (((z + dz) % zs) * YS + (y + dy) % YS, z * YS + y) for z in range(zs) for y in range(YS)
    ]
    return lax.ppermute(value, "seq", pairs)


def split_cols(value):
    half = -(-value.shape[-1] // (2 * LANES)) * LANES
    return value[..., :half], value[..., half:]


def shifted(axis):
    if axis == "z":
        return lambda value, step: receive(value, step, 0)
    return lambda value, step: receive(value, 0, step)


def direct_gather(own, axis, count):
    get = shifted(axis)
    return [own] + [get(own, step if step <= count // 2 else step - count) for step in range(1, count)]


def ring_gather(own, axis, count, halves):
    get = shifted(axis)
    blocks = [None] * count
    blocks[0] = own
    ahead = behind = own
    for lap in range(1, count // 2):
        ahead, behind = get(ahead, 1), get(behind, -1)
        blocks[lap], blocks[count - lap] = ahead, behind
    if halves:
        first, _ = split_cols(ahead)
        _, second = split_cols(behind)
        blocks[count // 2] = jnp.concatenate([get(first, 1), get(second, -1)], axis=-1)
    else:
        blocks[count // 2] = get(ahead, 1)
    return blocks


def add_rounded(left, right):
    return (left.astype(jnp.float32) + right.astype(jnp.float32)).astype(jnp.bfloat16)


def direct_reduce(blocks, axis):
    get = shifted(axis)
    count = len(blocks)
    total = blocks[0].astype(jnp.float32)
    for step in range(1, count):
        total = total + get(
            blocks[step], -step if step <= count // 2 else count - step
        ).astype(jnp.float32)
    return total.astype(jnp.bfloat16)


def ring_reduce(blocks, axis, halves):
    get = shifted(axis)
    count = len(blocks)
    middle = count // 2
    blocks = list(blocks)
    if halves:
        first, second = split_cols(blocks[middle])
        first, second = get(first, -1), get(second, 1)
        half = first.shape[-1]
        up, down = blocks[middle - 1], blocks[middle + 1]
        blocks[middle - 1] = jnp.concatenate(
            [add_rounded(up[..., :half], first), up[..., half:]], axis=-1
        )
        blocks[middle + 1] = jnp.concatenate(
            [down[..., :half], add_rounded(down[..., half:], second)], axis=-1
        )
    else:
        blocks[middle - 1] = add_rounded(blocks[middle - 1], get(blocks[middle], -1))
    first, second = blocks[middle - 1], blocks[middle + 1]
    for lap in range(middle - 1, 0, -1):
        first, second = get(first, -1), get(second, 1)
        if lap > 1:
            first = add_rounded(blocks[lap - 1], first)
            second = add_rounded(blocks[count - lap + 1], second)
    total = (
        blocks[0].astype(jnp.float32) + first.astype(jnp.float32) + second.astype(jnp.float32)
    )
    return total.astype(jnp.bfloat16)


def cut_of(width):
    return -(-width // (2 * LANES)) * LANES


def relayed_gather(own):
    get = shifted("z")
    one, back, two, behind = get(own, 1), get(own, -1), get(own, 2), get(own, -2)
    return [own, one, two, get(two, 1), get(two, 2), get(behind, -1), behind, back]


def relayed_reduce(blocks):
    get = shifted("z")
    four, three, less = get(blocks[4], -2), get(blocks[3], -1), get(blocks[5], 1)
    one, back = get(blocks[1], -1), get(blocks[7], 1)
    two = blocks[2].astype(jnp.float32) + four.astype(jnp.float32) + three.astype(jnp.float32)
    two = get(two.astype(jnp.bfloat16), -2)
    behind = get(add_rounded(blocks[6], less), 2)
    total = blocks[0].astype(jnp.float32)
    for other in (one, back, two, behind):
        total = total + other.astype(jnp.float32)
    return total.astype(jnp.bfloat16)


def gather_slots(rows):
    zs = lax.axis_size("seq") // YS
    cut = cut_of(rows.shape[-1])
    left = jnp.stack(direct_gather(rows[:, :cut], "y", YS))
    right = jnp.stack(relayed_gather(rows[:, cut:]))
    left = jnp.stack(ring_gather(left, "z", zs, False))
    right = jnp.stack(ring_gather(right, "y", YS, True), axis=1)
    return jnp.concatenate([left, right], axis=-1)


def reduce_slots(terms):
    zs = terms.shape[0]
    cut = cut_of(terms.shape[-1])
    left = ring_reduce([terms[dz, :, :, :cut] for dz in range(zs)], "z", False)
    right = ring_reduce([terms[:, dy, :, cut:] for dy in range(YS)], "y", True)
    left = direct_reduce([left[dy] for dy in range(YS)], "y")
    right = relayed_reduce([right[dz] for dz in range(zs)])
    return jnp.concatenate([left, right], axis=-1)


F32 = jnp.float32
BF16 = jnp.bfloat16

NT = (((1,), (1,)), ((), ()))
TN = (((0,), (0,)), ((), ()))
NN = (((1,), (0,)), ((), ()))


def mm(left, right, dims=NN):
    return lax.dot_general(left, right, dims, preferred_element_type=F32)


def parts_of(value):
    high = value.astype(BF16).astype(F32)
    middle = (value - high).astype(BF16).astype(F32)
    return high, middle, (value - high - middle).astype(BF16).astype(F32)


def by_half(left, right, low):
    return jnp.where(low, left, right)


def both_rows(rows, low):
    zero = jnp.zeros_like(rows)
    return jnp.concatenate([jnp.where(low, rows, zero), jnp.where(low, zero, rows)], axis=0)


def prepare_body(
    places_ref, keys_ref, values_ref, query_ref, decay_ref,
    payload_ref, lifted_ref, total_ref, tails_ref, lifts_ref, weights_ref, scores_ref, attended_ref, spread_ref,
):
    tokens, width = keys_ref.shape
    reads = query_ref.shape[0]
    heads = decay_ref.shape[0]
    pairs = heads // 2
    size = width // heads
    blocks, _, _ = payload_ref.shape
    rows = pairs * size // blocks
    decay = decay_ref[...]
    t0 = lax.broadcasted_iota(jnp.int32, (tokens, tokens), 0)
    t1 = lax.broadcasted_iota(jnp.int32, (tokens, tokens), 1)
    lower = (t1 <= t0).astype(F32)
    upper = (t0 <= t1).astype(F32)
    cum = sum(mm(part.astype(BF16), upper.astype(BF16)) for part in parts_of(decay))
    cum_t = sum(mm(lower.astype(BF16), part.astype(BF16), NT) for part in parts_of(decay))
    spread_ref[...] = cum_t
    total_ref[...] = cum_t[tokens - 1 : tokens]
    tail = jnp.exp(cum_t[tokens - 1 : tokens] - cum_t)
    tails_ref[...] = tail
    total = cum[:, tokens - 1 : tokens]
    at_read = jnp.concatenate([spread_ref[pl.ds(places_ref[r], 1), :] for r in range(reads)], axis=0)
    lift = jnp.exp(at_read)
    lifts_ref[...] = lift
    lane = lax.broadcasted_iota(jnp.int32, (1, LANES), 1)
    low = lane < size
    spot = lax.broadcasted_iota(jnp.int32, (reads, tokens), 1)
    row = lax.broadcasted_iota(jnp.int32, (reads, tokens), 0)
    place = jnp.zeros((reads, tokens), jnp.int32)
    for r in range(reads):
        place = jnp.where(row == r, places_ref[r], place)
    allowed = spot <= place
    lanes_total = []
    for p in range(pairs):
        cols = slice(p * LANES, (p + 1) * LANES)
        one, two = 2 * p, 2 * p + 1
        key, value, query = keys_ref[:, cols], values_ref[:, cols], query_ref[:, cols]
        fade = by_half(tail[:, one : one + 1], tail[:, two : two + 1], low)
        state = mm((key.astype(F32) * fade).astype(BF16), value, TN)
        state = by_half(state[:size], state[size:], low).astype(BF16)
        for chunk in range(size // 16):
            where = p * (size // 16) + chunk
            block, offset = where // (rows // 16), where % (rows // 16)
            payload_ref[block, offset * 16 : offset * 16 + 16, :] = state[chunk * 16 : chunk * 16 + 16]
        lanes_total.append(by_half(total[one : one + 1], total[two : two + 1], low))
        raised = by_half(lift[:, one : one + 1], lift[:, two : two + 1], low)
        lifted_ref[:, cols] = (query.astype(F32) * raised).astype(BF16)
        weight = [
            jnp.exp(jnp.where(allowed, at_read[:, h : h + 1] - cum[h : h + 1, :], -1e30))
            for h in (one, two)
        ]
        weight = jnp.concatenate(weight, axis=0)
        weights_ref[p] = weight
        score = weight * mm(both_rows(query, low), key, NT) * (1.0 / size)
        scores_ref[p] = score
        near = mm(score.astype(BF16), value)
        attended_ref[:, cols] = by_half(near[:reads], near[reads:], low)
    for block in range(blocks):
        first = block * rows // size
        last = (block * rows + rows - 1) // size
        meta = list(parts_of(lanes_total[first])) + list(parts_of(lanes_total[last]))
        meta = jnp.concatenate(meta + [jnp.zeros((2, LANES), F32)], axis=0)
        payload_ref[block, rows : rows + 8, :] = meta.astype(BF16)


def prepare(places, keys, values, query, decay, blocks):
    tokens, width = keys.shape
    reads = query.shape[0]
    heads = decay.shape[0]
    pairs = heads // 2
    rows = pairs * (width // heads) // blocks
    vmem = pl.BlockSpec(memory_space=pltpu.VMEM)
    return pl.pallas_call(
        prepare_body,
        out_shape=(
            jax.ShapeDtypeStruct((blocks, rows + 8, LANES), BF16),
            jax.ShapeDtypeStruct((reads, width), BF16),
            jax.ShapeDtypeStruct((1, heads), F32),
            jax.ShapeDtypeStruct((tokens, heads), F32),
            jax.ShapeDtypeStruct((reads, heads), F32),
            jax.ShapeDtypeStruct((pairs, 2 * reads, tokens), F32),
            jax.ShapeDtypeStruct((pairs, 2 * reads, tokens), F32),
            jax.ShapeDtypeStruct((reads, width), F32),
        ),
        in_specs=[pl.BlockSpec(memory_space=pltpu.SMEM)] + [vmem] * 4,
        out_specs=(vmem,) * 8,
        scratch_shapes=[pltpu.VMEM((tokens, heads), F32)],
        name="prepare",
    )(places, keys, values, query, decay)


def finish_body(
    place_ref, keys_ref, values_ref, query_ref, slope_ref, far_ref, parts_ref, state_ref, tails_ref,
    lifts_ref, weights_ref, scores_ref,
    keys_out, values_out, query_out,
):
    tokens, width = keys_ref.shape
    reads = query_ref.shape[0]
    heads = tails_ref.shape[1]
    pairs = heads // 2
    size = width // heads
    low = lax.broadcasted_iota(jnp.int32, (1, LANES), 1) < size
    r0 = lax.broadcasted_iota(jnp.int32, (LANES, LANES), 0) < size
    r1 = lax.broadcasted_iota(jnp.int32, (LANES, LANES), 1) < size
    same = r0 == r1
    tail, lift = tails_ref[...], lifts_ref[...]
    own, ys = place_ref[0], place_ref[1]
    blocks = parts_ref.shape[1]
    count = blocks * reads
    half = far_ref.shape[1] // 2

    def whose(step):
        return ((own // ys + step // ys) % (blocks // ys)) * ys + (own + step) % ys

    row = lax.broadcasted_iota(jnp.int32, (count, blocks), 0)
    other = whose(lax.broadcasted_iota(jnp.int32, (count, blocks), 1))
    mine = whose(row // reads)
    between = ((other > own) & (other < mine)).astype(BF16)
    reach = jnp.exp(mm(between, parts_ref[0]) + mm(between, parts_ref[1]) + mm(between, parts_ref[2]))
    reach = jnp.where(mine[:, :1] > own, reach, 0.0) * (1.0 / size)
    for p in range(pairs):
        cols = slice(p * LANES, (p + 1) * LANES)
        one, two = 2 * p, 2 * p + 1
        key, value, query = keys_ref[:, cols], values_ref[:, cols], query_ref[:, cols]
        slope = slope_ref[:, cols].astype(BF16)
        far = by_half(reach[:, one : one + 1], reach[:, two : two + 1], low)
        rows = far_ref[:, :half, cols].reshape(count, LANES)
        far = (far_ref[:, half:, cols].reshape(count, LANES).astype(F32) * far).astype(BF16)
        suffix = jnp.where(same, mm(far, rows, TN), 0.0).astype(BF16)
        fade = by_half(tail[:, one : one + 1], tail[:, two : two + 1], low)
        slopes = both_rows(slope, low)
        near = (weights_ref[p] * mm(slopes, value, NT) * (1.0 / size)).astype(BF16)
        keys_out[:, cols] = mm(near, both_rows(query, low), TN) + fade * mm(value, suffix, NT)
        values_out[:, cols] = mm(scores_ref[p].astype(BF16), slopes, TN) + fade * mm(key, suffix)
        state = state_ref[p]
        zero = jnp.zeros_like(state)
        state = jnp.concatenate([jnp.where(low, state, zero), jnp.where(low, zero, state)], axis=0)
        raised = by_half(lift[:, one : one + 1], lift[:, two : two + 1], low) * (1.0 / size)
        own = mm(near, key)
        query_out[:, cols] = by_half(own[:reads], own[reads:], low) + raised * mm(slope, state, NT)


def finish(place, keys, values, query, slope, far, parts, state, tails, lifts, weights, scores):
    tokens, width = keys.shape
    reads = query.shape[0]
    vmem = pl.BlockSpec(memory_space=pltpu.VMEM)
    return pl.pallas_call(
        finish_body,
        out_shape=(
            jax.ShapeDtypeStruct((tokens, width), F32),
            jax.ShapeDtypeStruct((tokens, width), F32),
            jax.ShapeDtypeStruct((reads, width), F32),
        ),
        in_specs=[pl.BlockSpec(memory_space=pltpu.SMEM)] + [vmem] * 11,
        out_specs=(vmem,) * 3,
        name="finish",
    )(place, keys, values, query, slope, far, parts, state, tails, lifts, weights, scores)


def targets(ids_ref, capacity):
    reads = ids_ref.shape[0]
    out = []
    for r in range(reads):
        mine = []
        for k in range(2):
            name = ids_ref[r, k]
            slot = name * capacity
            for q in range(r):
                slot = slot + (ids_ref[q, 0] == name).astype(jnp.int32)
                slot = slot + (ids_ref[q, 1] == name).astype(jnp.int32)
            mine.append(slot)
        out.append(mine)
    return out


def column(scalars):
    rows = lax.broadcasted_iota(jnp.int32, (len(scalars), 1), 0)
    out = jnp.zeros((len(scalars), 1), jnp.int32)
    for r, scalar in enumerate(scalars):
        out = jnp.where(rows == r, scalar, out)
    return out


def route_body(
    ids_ref, state_ref, query_ref, lifts_ref, attended_ref, resid_ref, gain_ref, router_ref, score_ref,
    out_ref, unit_ref, small_ref, residual_ref,
):
    reads, width = query_ref.shape
    heads = lifts_ref.shape[1]
    pairs = heads // 2
    size = width // heads
    slots = out_ref.shape[0]
    experts = router_ref.shape[0]
    capacity = slots // experts
    low = lax.broadcasted_iota(jnp.int32, (1, LANES), 1) < size
    lift = lifts_ref[...]
    square = jnp.zeros((reads, LANES), F32)
    for p in range(pairs):
        cols = slice(p * LANES, (p + 1) * LANES)
        one, two = 2 * p, 2 * p + 1
        state = state_ref[p]
        zero = jnp.zeros_like(state)
        state = jnp.concatenate([jnp.where(low, state, zero), jnp.where(low, zero, state)], axis=0)
        raised = by_half(lift[:, one : one + 1], lift[:, two : two + 1], low) * (1.0 / size)
        residual = (
            resid_ref[:, cols].astype(F32) + attended_ref[:, cols] + raised * mm(query_ref[:, cols], state)
        )
        residual_ref[:, cols] = residual
        square = square + residual * residual
    inverse = lax.rsqrt(jnp.sum(square, axis=1, keepdims=True) * (1.0 / width) + EPSILON)
    residual = residual_ref[...]
    unit = residual * inverse
    unit_ref[...] = unit
    normed = (unit * gain_ref[...].astype(F32)).astype(BF16)
    logits = mm(normed, router_ref[...], NT)
    names = lax.broadcasted_iota(jnp.int32, (1, experts), 1)
    chosen = [
        jnp.sum(
            jnp.where(names == column([ids_ref[r, k] for r in range(reads)]), logits, 0.0),
            axis=1,
            keepdims=True,
        )
        for k in range(2)
    ]
    first = jax.nn.sigmoid(chosen[0] - chosen[1])
    own = jnp.sum(residual * score_ref[...].astype(F32), axis=1, keepdims=True)
    lane = lax.broadcasted_iota(jnp.int32, (reads, LANES), 1)
    small_ref[...] = jnp.where(lane == 0, inverse, jnp.where(lane == 1, first, own))
    slot = lax.broadcasted_iota(jnp.int32, (slots, 1), 0)
    where = targets(ids_ref, capacity)
    normed = normed.astype(F32)
    out = jnp.zeros((slots, width), F32)
    for r in range(reads):
        out = jnp.where((slot == where[r][0]) | (slot == where[r][1]), normed[r : r + 1], out)
    out_ref[...] = out.astype(BF16)


def route(ids, state, query, lifts, attended, resid, gain, router, score, slots):
    reads, width = query.shape
    vmem = pl.BlockSpec(memory_space=pltpu.VMEM)
    return pl.pallas_call(
        route_body,
        out_shape=(
            jax.ShapeDtypeStruct((slots, width), BF16),
            jax.ShapeDtypeStruct((reads, width), F32),
            jax.ShapeDtypeStruct((reads, LANES), F32),
        ),
        in_specs=[pl.BlockSpec(memory_space=pltpu.SMEM)] + [vmem] * 8,
        out_specs=(vmem,) * 3,
        scratch_shapes=[pltpu.VMEM((reads, width), F32)],
        name="route",
    )(ids, state, query, lifts, attended, resid, gain, router, score)


def slope_body(
    ids_ref, returned_ref, unit_ref, small_ref, gain_ref, router_ref, score_ref, lifted_ref, total_ref,
    slope_ref, payload_ref,
):
    reads, width = unit_ref.shape
    slots = returned_ref.shape[0]
    experts = router_ref.shape[0]
    capacity = slots // experts
    where = targets(ids_ref, capacity)
    spots = [column([where[r][k] for r in range(reads)]) for k in range(2)]
    inverse, first, own = (small_ref[:, i : i + 1] for i in range(3))
    gates = (first, 1.0 - first)
    d_in = jnp.zeros((reads, width), F32)
    scores = [jnp.zeros((reads, 1), F32) for _ in range(2)]
    for slot in range(slots):
        row = returned_ref[slot : slot + 1, :width].astype(F32)
        told = returned_ref[slot : slot + 1, width : width + 1].astype(F32)
        weight = jnp.where(spots[0] == slot, gates[0], 0.0) + jnp.where(spots[1] == slot, gates[1], 0.0)
        d_in = d_in + weight * row
        scores = [s + jnp.where(spot == slot, told, 0.0) for s, spot in zip(scores, spots)]
    own = own + gates[0] * scores[0] + gates[1] * scores[1]
    d_logit = (scores[0] - scores[1]) * gates[0] * gates[1]
    columns = jnp.zeros((reads, width), F32)
    picks = [column([ids_ref[r, k] for r in range(reads)]) for k in range(2)]
    for name in range(experts):
        sign = (picks[0] == name).astype(F32) - (picks[1] == name).astype(F32)
        columns = columns + sign * router_ref[name : name + 1, :].astype(F32)
    d_unit = (d_in + d_logit * columns) * gain_ref[...].astype(F32)
    unit = unit_ref[...]
    mean = jnp.sum(d_unit * unit, axis=1, keepdims=True) * (1.0 / width)
    slope = score_ref[...].astype(F32) + inverse * (d_unit - unit * mean)
    slope_ref[...] = slope
    payload_ref[:, :width] = jnp.concatenate([slope, lifted_ref[...].astype(F32)], axis=0).astype(BF16)
    heads = total_ref.shape[1]
    lane = lax.broadcasted_iota(jnp.int32, (1, LANES), 1)
    total = jnp.concatenate(
        list(parts_of(total_ref[...])) + [jnp.zeros((1, heads), F32)], axis=0
    )
    total = jnp.concatenate([total, jnp.zeros((4, LANES - heads), F32)], axis=1)
    high, middle, rest = parts_of(jnp.sum(own, axis=0, keepdims=True))
    told = jnp.where(lane == 0, high, jnp.where(lane == 1, middle, jnp.where(lane == 2, rest, 0.0)))
    row = lax.broadcasted_iota(jnp.int32, (4, LANES), 0)
    meta = jnp.where(row == 3, told, total)
    payload_ref[:, width:] = jnp.concatenate([meta, jnp.zeros((4, LANES), F32)], axis=0).astype(BF16)


def slope_of(ids, returned, unit, small, gain, router, score, lifted, total):
    reads, width = unit.shape
    vmem = pl.BlockSpec(memory_space=pltpu.VMEM)
    return pl.pallas_call(
        slope_body,
        out_shape=(
            jax.ShapeDtypeStruct((reads, width), F32),
            jax.ShapeDtypeStruct((2 * reads, width + LANES), BF16),
        ),
        in_specs=[pl.BlockSpec(memory_space=pltpu.SMEM)] + [vmem] * 8,
        out_specs=(vmem,) * 2,
        name="slope",
    )(ids, returned, unit, small, gain, router, score, lifted, total)


def share_body(place_ref, meta_ref, out_ref):
    blocks = meta_ref.shape[0]
    ys = place_ref[1]
    own = place_ref[0]
    step = lax.broadcasted_iota(jnp.int32, (blocks, LANES), 0)
    lane = lax.broadcasted_iota(jnp.int32, (blocks, LANES), 1)
    whose = ((own // ys + step // ys) % (blocks // ys)) * ys + (own + step) % ys
    told = jnp.sum(jnp.where(lane < 3, meta_ref[...].astype(F32), 0.0), axis=1, keepdims=True)
    line = jnp.sum(jnp.where(whose == lane, told, 0.0), axis=0, keepdims=True)
    out_ref[...] = jnp.broadcast_to(jnp.sum(line, axis=1, keepdims=True), out_ref.shape)


def share(place, meta, copies):
    return pl.pallas_call(
        share_body,
        out_shape=jax.ShapeDtypeStruct((copies, LANES), F32),
        in_specs=[pl.BlockSpec(memory_space=pltpu.SMEM), pl.BlockSpec(memory_space=pltpu.VMEM)],
        out_specs=pl.BlockSpec(memory_space=pltpu.VMEM),
        name="share",
    )(place, meta)


def scale_body(
    place_ref, order_ref, lengths_ref, sums_ref, keys_ref, values_ref, query_ref, slope_ref,
    loss_ref, query_out, slope_out, keys_out, values_out, *, span, rows, length_weight, score_scale,
):
    count = sums_ref.shape[0]
    reward = sums_ref[...] * (1.0 / rows)
    sub = lax.broadcasted_iota(jnp.int32, (count, LANES), 0)
    lane = lax.broadcasted_iota(jnp.int32, (count, LANES), 1)
    line = jnp.sum(jnp.where(sub == lane, reward, 0.0), axis=0, keepdims=True)
    live = (lax.broadcasted_iota(jnp.int32, (1, LANES), 1) < count).astype(F32)
    share = jnp.zeros((1, LANES), F32)
    for i in range(count):
        share = jnp.where(lane[:1] == i, lengths_ref[i].astype(F32), share)
    share = share * (1.0 / span)
    fitted = jnp.zeros((1, 1), F32)
    slope = jnp.zeros((1, LANES), F32)
    for pair in range(count // 2):
        better, worse = order_ref[2 * pair], order_ref[2 * pair + 1]
        gap = jnp.sum(
            jnp.where(lane[:1] == worse, line, 0.0) - jnp.where(lane[:1] == better, line, 0.0),
            axis=1,
            keepdims=True,
        )
        fitted = fitted + jnp.maximum(gap, 0.0) + jnp.log1p(jnp.exp(-jnp.abs(gap)))
        pull = jax.nn.sigmoid(gap) * (2.0 / count)
        slope = slope + jnp.where(lane[:1] == worse, pull, 0.0) - jnp.where(lane[:1] == better, pull, 0.0)
    def mean(x):
        return jnp.sum(x * live, axis=1, keepdims=True) * (1.0 / count)
    lean = (share - mean(share)) * live
    both = mean((line - mean(line)) * lean)
    loss_ref[...] = jnp.broadcast_to(fitted * (2.0 / count) + length_weight * both * both, loss_ref.shape)
    slope = slope + (2.0 * length_weight / count) * both * (lean - mean(lean))
    factor = jnp.sum(jnp.where(lane[:1] == place_ref[0], slope, 0.0), axis=1, keepdims=True) * score_scale
    query_out[...] = query_ref[...] * factor
    slope_out[...] = slope_ref[...] * factor
    keys_out[...] = (keys_ref[...] * factor).astype(BF16)
    values_out[...] = (values_ref[...] * factor).astype(BF16)


def scale(place, order, lengths, sums, keys, values, query, slope, **sizes):
    smem, vmem = pl.BlockSpec(memory_space=pltpu.SMEM), pl.BlockSpec(memory_space=pltpu.VMEM)
    tokens, width = keys.shape
    reads = query.shape[0]
    return pl.pallas_call(
        functools.partial(scale_body, **sizes),
        out_shape=(
            jax.ShapeDtypeStruct((1, 1), F32),
            jax.ShapeDtypeStruct((reads, width), F32),
            jax.ShapeDtypeStruct((reads, width), F32),
            jax.ShapeDtypeStruct((tokens, width), BF16),
            jax.ShapeDtypeStruct((tokens, width), BF16),
        ),
        in_specs=[smem] * 3 + [vmem] * 5,
        out_specs=(vmem,) * 5,
        name="scale",
    )(place, order, lengths, sums, keys, values, query, slope)


def arrange_body(*refs):
    out_ref = refs[-1]
    half = refs[0].shape[0] // 2
    blocks = [ref[...].astype(F32) for ref in refs[:-1]]
    rows = [block[:half] for block in blocks] + [block[half:] for block in blocks]
    out_ref[...] = jnp.concatenate(rows, axis=0).astype(BF16)


def arrange(blocks):
    rows, width = blocks[0].shape
    vmem = pl.BlockSpec(memory_space=pltpu.VMEM)
    return pl.pallas_call(
        arrange_body,
        out_shape=jax.ShapeDtypeStruct((rows * len(blocks), width), BF16),
        in_specs=[vmem] * len(blocks),
        out_specs=vmem,
        name="arrange",
    )(*blocks)


def prefix_body(bound_ref, terms_ref, out_ref):
    blocks, rows, lanes = out_ref.shape
    near = lax.broadcasted_iota(jnp.int32, (rows, lanes), 0) < bound_ref[0]
    state = jnp.zeros((rows, lanes), jnp.float32)
    for block in range(blocks):
        out_ref[block] = state.astype(jnp.bfloat16)
        tail = terms_ref[block, rows : rows + 8, :].astype(jnp.float32)
        one = jnp.exp(tail[0:1] + tail[1:2] + tail[2:3])
        two = jnp.exp(tail[3:4] + tail[4:5] + tail[5:6])
        state = state * jnp.where(near, one, two) + terms_ref[block, :rows, :].astype(jnp.float32)

def exclusive_states(payload):
    count, rows, lanes = payload.shape
    rows = rows - 8
    size = lanes // 2
    place = lax.axis_index("seq")
    arrived = lax.all_to_all(payload, "seq", 0, 0, tiled=True)
    bound = ((place * rows) // size + 1) * size - place * rows
    vmem = pl.BlockSpec(memory_space=pltpu.VMEM)
    sums = pl.pallas_call(
        prefix_body,
        out_shape=jax.ShapeDtypeStruct((count, rows, lanes), BF16),
        in_specs=[pl.BlockSpec(memory_space=pltpu.SMEM), vmem],
        out_specs=vmem,
        name="state_prefix",
    )(bound.reshape(1), arrived)
    back = lax.all_to_all(sums, "seq", 0, 0, tiled=True)
    return back.reshape(count * rows // size, size, lanes)


def per_device(
    resid_rows,
    query_rows,
    key_rows,
    value_rows,
    log_decay,
    read_pos,
    expert_ids,
    pair_order,
    lengths,
    norm_gain,
    router_weight,
    score_weight,
    gate_weight,
    up_weight,
    down_weight,
):
    seq_count = lax.axis_size("seq")
    exp_count = lax.axis_size("exp")
    seq_index = lax.axis_index("seq")
    exp_index = lax.axis_index("exp")
    zs = seq_count // YS
    token_count = key_rows.shape[1]
    model_width = key_rows.shape[2]
    read_count = query_rows.shape[1]
    expert_count = router_weight.shape[1]
    capacity = max(2, 4 * read_count // exp_count)
    slot_count = expert_count * capacity
    wide = model_width + LANES
    keys, values, query = key_rows[0], value_rows[0], query_rows[0]
    ids = expert_ids[0].astype(jnp.int32)
    gain = norm_gain.reshape(1, model_width)
    score = score_weight.reshape(1, model_width)
    router = router_weight.T
    place = jnp.stack([seq_index, jnp.int32(YS)]).astype(jnp.int32)

    payload, lifted, total, tails, lifts, weights, scores, attended = prepare(
        read_pos[0] - seq_index * token_count, keys, values, query, log_decay[0], seq_count
    )
    state = exclusive_states(payload)
    outgoing, unit, small = route(
        ids, state, query, lifts, attended, resid_rows[0], gain, router, score, slot_count
    )
    arrived = lax.all_to_all(
        outgoing.reshape(expert_count, capacity, model_width), "exp", 0, 0, tiled=True
    ).reshape(slot_count, model_width)
    piece = gather_slots(arrived).reshape(seq_count * slot_count, model_width)

    gate_w = gate_weight[0]
    up_w = up_weight[0]
    down_w = down_weight[0]
    down_score = jnp.sum(down_w.astype(F32) * score.astype(F32), axis=1)
    pre_gate = jnp.dot(piece, gate_w, preferred_element_type=F32)
    pre_up = jnp.dot(piece, up_w, preferred_element_type=F32)
    gate_sigmoid = jax.nn.sigmoid(pre_gate)
    silu = pre_gate * gate_sigmoid
    slot_score = jnp.sum(silu * pre_up * down_score[None, :], axis=1)
    d_pre_gate = (
        down_score[None, :] * pre_up * gate_sigmoid * (1.0 + pre_gate * (1.0 - gate_sigmoid))
    ).astype(BF16)
    d_pre_up = (down_score[None, :] * silu).astype(BF16)
    back = jnp.einsum("sf,df->sd", d_pre_gate, gate_w, preferred_element_type=F32)
    back = back + jnp.einsum("sf,df->sd", d_pre_up, up_w, preferred_element_type=F32)
    score_cols = jnp.pad(slot_score[:, None], ((0, 0), (0, LANES - 1)))
    terms = jnp.concatenate([back, score_cols], axis=1).astype(BF16)
    summed = reduce_slots(terms.reshape(zs, YS, slot_count, wide))
    returned = lax.all_to_all(
        summed.reshape(expert_count, capacity, wide), "exp", 0, 0, tiled=True
    ).reshape(slot_count, wide)

    slope, rows = slope_of(ids, returned, unit, small, gain, router, score, lifted, total)
    rows = arrange(direct_gather(rows, "y", YS))
    rows = jnp.stack(ring_gather(rows, "z", zs, False))
    meta = rows[:, : YS * read_count, model_width:].reshape(seq_count, read_count, LANES)
    sums = share(place, meta[:, 3], exp_count)
    sums = lax.all_to_all(sums.reshape(exp_count, 1, LANES), "exp", 0, 0, tiled=True)
    parts = meta[:, :3].transpose(1, 0, 2)
    grad_keys, grad_values, grad_query = finish(
        place, keys, values, query, slope, rows, parts, state, tails, lifts, weights, scores
    )
    loss, grad_query, grad_resid, grad_keys, grad_values = scale(
        exp_index.reshape(1).astype(jnp.int32),
        pair_order,
        lengths,
        sums.reshape(exp_count, LANES),
        grad_keys,
        grad_values,
        grad_query,
        slope,
        span=token_count * seq_count,
        rows=read_count * seq_count,
        length_weight=LENGTH_WEIGHT,
        score_scale=SCORE_SCALE,
    )
    return (loss.reshape(()), grad_query[None], grad_resid[None], grad_keys[None], grad_values[None])


def solution(mesh):
    in_specs = (
        P("exp", "seq", None),
        P("exp", "seq", None),
        P("exp", "seq", None),
        P("exp", "seq", None),
        P("exp", None, "seq"),
        P("exp", "seq"),
        P("exp", "seq", None),
        P(),
        P(),
        P(),
        P(),
        P(),
        P("exp", None, "seq"),
        P("exp", None, "seq"),
        P("exp", "seq", None),
    )
    out_specs = (
        P(),
        P("exp", "seq", None),
        P("exp", "seq", None),
        P("exp", "seq", None),
        P("exp", "seq", None),
    )
    return jax.shard_map(
        per_device, mesh=mesh, in_specs=in_specs, out_specs=out_specs, check_vma=False
    )
```

```python
import functools

import jax
import jax.numpy as jnp
import numpy as np
from jax import lax
from jax.experimental import pallas as pl
from jax.experimental.pallas import tpu as pltpu
from jax.sharding import PartitionSpec as P

EPSILON = 1e-06
LENGTH_WEIGHT = 4.0
SCORE_SCALE = 256.0
YS = 4
LANES = 128


def receive(value, dz, dy):
    zs = lax.axis_size("seq") // YS
    pairs = [
        (((z + dz) % zs) * YS + (y + dy) % YS, z * YS + y) for z in range(zs) for y in range(YS)
    ]
    return lax.ppermute(value, "seq", pairs)


def split_cols(value):
    half = -(-value.shape[-1] // (2 * LANES)) * LANES
    return value[..., :half], value[..., half:]


def shifted(axis):
    if axis == "z":
        return lambda value, step: receive(value, step, 0)
    return lambda value, step: receive(value, 0, step)


def direct_gather(own, axis, count):
    get = shifted(axis)
    return [own] + [get(own, step if step <= count // 2 else step - count) for step in range(1, count)]


def ring_gather(own, axis, count, halves):
    get = shifted(axis)
    blocks = [None] * count
    blocks[0] = own
    ahead = behind = own
    for lap in range(1, count // 2):
        ahead, behind = get(ahead, 1), get(behind, -1)
        blocks[lap], blocks[count - lap] = ahead, behind
    if halves:
        first, _ = split_cols(ahead)
        _, second = split_cols(behind)
        blocks[count // 2] = jnp.concatenate([get(first, 1), get(second, -1)], axis=-1)
    else:
        blocks[count // 2] = get(ahead, 1)
    return blocks


def add_rounded(left, right):
    return (left.astype(jnp.float32) + right.astype(jnp.float32)).astype(jnp.bfloat16)


def direct_reduce(blocks, axis):
    get = shifted(axis)
    count = len(blocks)
    total = blocks[0].astype(jnp.float32)
    for step in range(1, count):
        total = total + get(
            blocks[step], -step if step <= count // 2 else count - step
        ).astype(jnp.float32)
    return total.astype(jnp.bfloat16)


def ring_reduce(blocks, axis, halves):
    get = shifted(axis)
    count = len(blocks)
    middle = count // 2
    blocks = list(blocks)
    if halves:
        first, second = split_cols(blocks[middle])
        first, second = get(first, -1), get(second, 1)
        half = first.shape[-1]
        up, down = blocks[middle - 1], blocks[middle + 1]
        blocks[middle - 1] = jnp.concatenate(
            [add_rounded(up[..., :half], first), up[..., half:]], axis=-1
        )
        blocks[middle + 1] = jnp.concatenate(
            [down[..., :half], add_rounded(down[..., half:], second)], axis=-1
        )
    else:
        blocks[middle - 1] = add_rounded(blocks[middle - 1], get(blocks[middle], -1))
    first, second = blocks[middle - 1], blocks[middle + 1]
    for lap in range(middle - 1, 0, -1):
        first, second = get(first, -1), get(second, 1)
        if lap > 1:
            first = add_rounded(blocks[lap - 1], first)
            second = add_rounded(blocks[count - lap + 1], second)
    total = (
        blocks[0].astype(jnp.float32) + first.astype(jnp.float32) + second.astype(jnp.float32)
    )
    return total.astype(jnp.bfloat16)


def cut_of(width):
    return -(-width // (2 * LANES)) * LANES


def relayed_gather(own):
    get = shifted("z")
    one, back, two, behind = get(own, 1), get(own, -1), get(own, 2), get(own, -2)
    return [own, one, two, get(two, 1), get(two, 2), get(behind, -1), behind, back]


def relayed_reduce(blocks):
    get = shifted("z")
    four, three, less = get(blocks[4], -2), get(blocks[3], -1), get(blocks[5], 1)
    one, back = get(blocks[1], -1), get(blocks[7], 1)
    two = blocks[2].astype(jnp.float32) + four.astype(jnp.float32) + three.astype(jnp.float32)
    two = get(two.astype(jnp.bfloat16), -2)
    behind = get(add_rounded(blocks[6], less), 2)
    total = blocks[0].astype(jnp.float32)
    for other in (one, back, two, behind):
        total = total + other.astype(jnp.float32)
    return total.astype(jnp.bfloat16)


def gather_slots(rows):
    zs = lax.axis_size("seq") // YS
    cut = cut_of(rows.shape[-1])
    left = jnp.stack(direct_gather(rows[:, :cut], "y", YS))
    right = jnp.stack(relayed_gather(rows[:, cut:]))
    left = jnp.stack(ring_gather(left, "z", zs, False))
    right = jnp.stack(ring_gather(right, "y", YS, True), axis=1)
    return jnp.concatenate([left, right], axis=-1)


def reduce_slots(terms):
    zs = terms.shape[0]
    cut = cut_of(terms.shape[-1])
    left = ring_reduce([terms[dz, :, :, :cut] for dz in range(zs)], "z", False)
    right = ring_reduce([terms[:, dy, :, cut:] for dy in range(YS)], "y", True)
    left = direct_reduce([left[dy] for dy in range(YS)], "y")
    right = relayed_reduce([right[dz] for dz in range(zs)])
    return jnp.concatenate([left, right], axis=-1)


F32 = jnp.float32
BF16 = jnp.bfloat16

NT = (((1,), (1,)), ((), ()))
TN = (((0,), (0,)), ((), ()))
NN = (((1,), (0,)), ((), ()))


def mm(left, right, dims=NN):
    return lax.dot_general(left, right, dims, preferred_element_type=F32)


def parts_of(value):
    high = value.astype(BF16).astype(F32)
    middle = (value - high).astype(BF16).astype(F32)
    return high, middle, (value - high - middle).astype(BF16).astype(F32)


def by_half(left, right, low):
    return jnp.where(low, left, right)


def both_rows(rows, low):
    zero = jnp.zeros_like(rows)
    return jnp.concatenate([jnp.where(low, rows, zero), jnp.where(low, zero, rows)], axis=0)


def prepare_body(
    places_ref, keys_ref, values_ref, query_ref, decay_ref,
    payload_ref, lifted_ref, total_ref, tails_ref, lifts_ref, weights_ref, scores_ref, attended_ref, spread_ref,
):
    tokens, width = keys_ref.shape
    reads = query_ref.shape[0]
    heads = decay_ref.shape[0]
    pairs = heads // 2
    size = width // heads
    blocks, _, _ = payload_ref.shape
    rows = pairs * size // blocks
    decay = decay_ref[...]
    t0 = lax.broadcasted_iota(jnp.int32, (tokens, tokens), 0)
    t1 = lax.broadcasted_iota(jnp.int32, (tokens, tokens), 1)
    lower = (t1 <= t0).astype(F32)
    upper = (t0 <= t1).astype(F32)
    cum = sum(mm(part.astype(BF16), upper.astype(BF16)) for part in parts_of(decay))
    cum_t = sum(mm(lower.astype(BF16), part.astype(BF16), NT) for part in parts_of(decay))
    spread_ref[...] = cum_t
    total_ref[...] = cum_t[tokens - 1 : tokens]
    tail = jnp.exp(cum_t[tokens - 1 : tokens] - cum_t)
    tails_ref[...] = tail
    total = cum[:, tokens - 1 : tokens]
    at_read = jnp.concatenate([spread_ref[pl.ds(places_ref[r], 1), :] for r in range(reads)], axis=0)
    lift = jnp.exp(at_read)
    lifts_ref[...] = lift
    lane = lax.broadcasted_iota(jnp.int32, (1, LANES), 1)
    low = lane < size
    spot = lax.broadcasted_iota(jnp.int32, (reads, tokens), 1)
    row = lax.broadcasted_iota(jnp.int32, (reads, tokens), 0)
    place = jnp.zeros((reads, tokens), jnp.int32)
    for r in range(reads):
        place = jnp.where(row == r, places_ref[r], place)
    allowed = spot <= place
    lanes_total = []
    for p in range(pairs):
        cols = slice(p * LANES, (p + 1) * LANES)
        one, two = 2 * p, 2 * p + 1
        key, value, query = keys_ref[:, cols], values_ref[:, cols], query_ref[:, cols]
        fade = by_half(tail[:, one : one + 1], tail[:, two : two + 1], low)
        state = mm((key.astype(F32) * fade).astype(BF16), value, TN)
        state = by_half(state[:size], state[size:], low).astype(BF16)
        for chunk in range(size // 16):
            where = p * (size // 16) + chunk
            block, offset = where // (rows // 16), where % (rows // 16)
            payload_ref[block, offset * 16 : offset * 16 + 16, :] = state[chunk * 16 : chunk * 16 + 16]
        lanes_total.append(by_half(total[one : one + 1], total[two : two + 1], low))
        raised = by_half(lift[:, one : one + 1], lift[:, two : two + 1], low)
        lifted_ref[:, cols] = (query.astype(F32) * raised).astype(BF16)
        weight = [
            jnp.exp(jnp.where(allowed, at_read[:, h : h + 1] - cum[h : h + 1, :], -1e30))
            for h in (one, two)
        ]
        weight = jnp.concatenate(weight, axis=0)
        weights_ref[p] = weight
        score = weight * mm(both_rows(query, low), key, NT) * (1.0 / size)
        scores_ref[p] = score
        near = mm(score.astype(BF16), value)
        attended_ref[:, cols] = by_half(near[:reads], near[reads:], low)
    for block in range(blocks):
        first = block * rows // size
        last = (block * rows + rows - 1) // size
        meta = list(parts_of(lanes_total[first])) + list(parts_of(lanes_total[last]))
        meta = jnp.concatenate(meta + [jnp.zeros((2, LANES), F32)], axis=0)
        payload_ref[block, rows : rows + 8, :] = meta.astype(BF16)


def prepare(places, keys, values, query, decay, blocks):
    tokens, width = keys.shape
    reads = query.shape[0]
    heads = decay.shape[0]
    pairs = heads // 2
    rows = pairs * (width // heads) // blocks
    vmem = pl.BlockSpec(memory_space=pltpu.VMEM)
    return pl.pallas_call(
        prepare_body,
        out_shape=(
            jax.ShapeDtypeStruct((blocks, rows + 8, LANES), BF16),
            jax.ShapeDtypeStruct((reads, width), BF16),
            jax.ShapeDtypeStruct((1, heads), F32),
            jax.ShapeDtypeStruct((tokens, heads), F32),
            jax.ShapeDtypeStruct((reads, heads), F32),
            jax.ShapeDtypeStruct((pairs, 2 * reads, tokens), F32),
            jax.ShapeDtypeStruct((pairs, 2 * reads, tokens), F32),
            jax.ShapeDtypeStruct((reads, width), F32),
        ),
        in_specs=[pl.BlockSpec(memory_space=pltpu.SMEM)] + [vmem] * 4,
        out_specs=(vmem,) * 8,
        scratch_shapes=[pltpu.VMEM((tokens, heads), F32)],
        name="prepare",
    )(places, keys, values, query, decay)


def loss_terms(line, place, order_ref, lengths_ref, span, length_weight):
    count = order_ref.shape[0]
    lane = lax.broadcasted_iota(jnp.int32, (1, LANES), 1)
    live = (lax.broadcasted_iota(jnp.int32, (1, LANES), 1) < count).astype(F32)
    share = jnp.zeros((1, LANES), F32)
    for i in range(count):
        share = jnp.where(lane == i, lengths_ref[i].astype(F32), share)
    share = share * (1.0 / span)
    fitted = jnp.zeros((1, 1), F32)
    slope = jnp.zeros((1, LANES), F32)
    for pair in range(count // 2):
        better, worse = order_ref[2 * pair], order_ref[2 * pair + 1]
        gap = jnp.sum(
            jnp.where(lane == worse, line, 0.0) - jnp.where(lane == better, line, 0.0),
            axis=1,
            keepdims=True,
        )
        fitted = fitted + jnp.maximum(gap, 0.0) + jnp.log1p(jnp.exp(-jnp.abs(gap)))
        pull = jax.nn.sigmoid(gap) * (2.0 / count)
        slope = slope + jnp.where(lane == worse, pull, 0.0) - jnp.where(lane == better, pull, 0.0)
    def mean(x):
        return jnp.sum(x * live, axis=1, keepdims=True) * (1.0 / count)
    lean = (share - mean(share)) * live
    both = mean((line - mean(line)) * lean)
    loss = fitted * (2.0 / count) + length_weight * both * both
    slope = slope + (2.0 * length_weight / count) * both * (lean - mean(lean))
    return loss, jnp.sum(jnp.where(lane == place, slope, 0.0), axis=1, keepdims=True)


def finish_body(
    place_ref, order_ref, lengths_ref,
    keys_ref, values_ref, query_ref, slope_ref, far_ref, parts_ref, state_ref, tails_ref,
    lifts_ref, weights_ref, scores_ref,
    loss_ref, query_out, slope_out, keys_out, values_out, *, span, length_weight, score_scale,
):
    tokens, width = keys_ref.shape
    reads = query_ref.shape[0]
    heads = tails_ref.shape[1]
    pairs = heads // 2
    size = width // heads
    low = lax.broadcasted_iota(jnp.int32, (1, LANES), 1) < size
    r0 = lax.broadcasted_iota(jnp.int32, (LANES, LANES), 0) < size
    r1 = lax.broadcasted_iota(jnp.int32, (LANES, LANES), 1) < size
    same = r0 == r1
    tail, lift = tails_ref[...], lifts_ref[...]
    own, ys = place_ref[0], place_ref[1]
    blocks = parts_ref.shape[1]
    count = blocks * reads
    half = far_ref.shape[1] // 2

    def whose(step):
        return ((own // ys + step // ys) % (blocks // ys)) * ys + (own + step) % ys

    experts = order_ref.shape[0]
    spot = lax.broadcasted_iota(jnp.int32, (blocks, blocks), 0)
    from_block = whose(lax.broadcasted_iota(jnp.int32, (blocks, blocks), 1))
    told = mm((spot == from_block).astype(BF16), parts_ref[3])
    told = jnp.sum(told, axis=0, keepdims=True) * (1.0 / count)
    line = told + pltpu.roll(told, LANES - experts, 1) + pltpu.roll(told, LANES - 2 * experts, 1)
    loss, factor = loss_terms(line, place_ref[2], order_ref, lengths_ref, span, length_weight)
    loss_ref[...] = loss
    factor = factor * score_scale
    slope_out[...] = slope_ref[...] * factor

    row = lax.broadcasted_iota(jnp.int32, (count, blocks), 0)
    other = whose(lax.broadcasted_iota(jnp.int32, (count, blocks), 1))
    mine = whose(row // reads)
    between = ((other > own) & (other < mine)).astype(BF16)
    reach = jnp.exp(mm(between, parts_ref[0]) + mm(between, parts_ref[1]) + mm(between, parts_ref[2]))
    reach = jnp.where(mine[:, :1] > own, reach, 0.0) * (1.0 / size)
    for p in range(pairs):
        cols = slice(p * LANES, (p + 1) * LANES)
        one, two = 2 * p, 2 * p + 1
        key, value, query = keys_ref[:, cols], values_ref[:, cols], query_ref[:, cols]
        slope = slope_ref[:, cols].astype(BF16)
        far = by_half(reach[:, one : one + 1], reach[:, two : two + 1], low)
        rows = far_ref[:, :half, cols].reshape(count, LANES)
        far = (far_ref[:, half:, cols].reshape(count, LANES).astype(F32) * far).astype(BF16)
        suffix = jnp.where(same, mm(far, rows, TN), 0.0).astype(BF16)
        fade = by_half(tail[:, one : one + 1], tail[:, two : two + 1], low)
        slopes = both_rows(slope, low)
        near = (weights_ref[p] * mm(slopes, value, NT) * (1.0 / size)).astype(BF16)
        grad = mm(near, both_rows(query, low), TN) + fade * mm(value, suffix, NT)
        keys_out[:, cols] = (grad * factor).astype(BF16)
        grad = mm(scores_ref[p].astype(BF16), slopes, TN) + fade * mm(key, suffix)
        values_out[:, cols] = (grad * factor).astype(BF16)
        state = state_ref[p]
        zero = jnp.zeros_like(state)
        state = jnp.concatenate([jnp.where(low, state, zero), jnp.where(low, zero, state)], axis=0)
        raised = by_half(lift[:, one : one + 1], lift[:, two : two + 1], low) * (1.0 / size)
        own = mm(near, key)
        grad = by_half(own[:reads], own[reads:], low) + raised * mm(slope, state, NT)
        query_out[:, cols] = grad * factor


def finish(place, order, lengths, keys, values, *rest, **sizes):
    tokens, width = keys.shape
    reads = rest[0].shape[0]
    smem, vmem = pl.BlockSpec(memory_space=pltpu.SMEM), pl.BlockSpec(memory_space=pltpu.VMEM)
    return pl.pallas_call(
        functools.partial(finish_body, **sizes),
        out_shape=(
            jax.ShapeDtypeStruct((1, 1), F32),
            jax.ShapeDtypeStruct((reads, width), F32),
            jax.ShapeDtypeStruct((reads, width), F32),
            jax.ShapeDtypeStruct((tokens, width), BF16),
            jax.ShapeDtypeStruct((tokens, width), BF16),
        ),
        in_specs=[smem] * 3 + [vmem] * (2 + len(rest)),
        out_specs=(vmem,) * 5,
        name="finish",
    )(place, order, lengths, keys, values, *rest)


def targets(ids_ref, capacity):
    reads = ids_ref.shape[0]
    out = []
    for r in range(reads):
        mine = []
        for k in range(2):
            name = ids_ref[r, k]
            slot = name * capacity
            for q in range(r):
                slot = slot + (ids_ref[q, 0] == name).astype(jnp.int32)
                slot = slot + (ids_ref[q, 1] == name).astype(jnp.int32)
            mine.append(slot)
        out.append(mine)
    return out


def column(scalars):
    rows = lax.broadcasted_iota(jnp.int32, (len(scalars), 1), 0)
    out = jnp.zeros((len(scalars), 1), jnp.int32)
    for r, scalar in enumerate(scalars):
        out = jnp.where(rows == r, scalar, out)
    return out


def route_body(
    ids_ref, state_ref, query_ref, lifts_ref, attended_ref, resid_ref, gain_ref, router_ref, score_ref,
    out_ref, unit_ref, small_ref, residual_ref,
):
    reads, width = query_ref.shape
    heads = lifts_ref.shape[1]
    pairs = heads // 2
    size = width // heads
    slots = out_ref.shape[0]
    experts = router_ref.shape[0]
    capacity = slots // experts
    low = lax.broadcasted_iota(jnp.int32, (1, LANES), 1) < size
    lift = lifts_ref[...]
    square = jnp.zeros((reads, LANES), F32)
    for p in range(pairs):
        cols = slice(p * LANES, (p + 1) * LANES)
        one, two = 2 * p, 2 * p + 1
        state = state_ref[p]
        zero = jnp.zeros_like(state)
        state = jnp.concatenate([jnp.where(low, state, zero), jnp.where(low, zero, state)], axis=0)
        raised = by_half(lift[:, one : one + 1], lift[:, two : two + 1], low) * (1.0 / size)
        residual = (
            resid_ref[:, cols].astype(F32) + attended_ref[:, cols] + raised * mm(query_ref[:, cols], state)
        )
        residual_ref[:, cols] = residual
        square = square + residual * residual
    inverse = lax.rsqrt(jnp.sum(square, axis=1, keepdims=True) * (1.0 / width) + EPSILON)
    residual = residual_ref[...]
    unit = residual * inverse
    unit_ref[...] = unit
    normed = (unit * gain_ref[...].astype(F32)).astype(BF16)
    logits = mm(normed, router_ref[...], NT)
    names = lax.broadcasted_iota(jnp.int32, (1, experts), 1)
    chosen = [
        jnp.sum(
            jnp.where(names == column([ids_ref[r, k] for r in range(reads)]), logits, 0.0),
            axis=1,
            keepdims=True,
        )
        for k in range(2)
    ]
    first = jax.nn.sigmoid(chosen[0] - chosen[1])
    own = jnp.sum(residual * score_ref[...].astype(F32), axis=1, keepdims=True)
    lane = lax.broadcasted_iota(jnp.int32, (reads, LANES), 1)
    small_ref[...] = jnp.where(lane == 0, inverse, jnp.where(lane == 1, first, own))
    slot = lax.broadcasted_iota(jnp.int32, (slots, 1), 0)
    where = targets(ids_ref, capacity)
    normed = normed.astype(F32)
    out = jnp.zeros((slots, width), F32)
    for r in range(reads):
        out = jnp.where((slot == where[r][0]) | (slot == where[r][1]), normed[r : r + 1], out)
    out_ref[...] = out.astype(BF16)


def route(ids, state, query, lifts, attended, resid, gain, router, score, slots):
    reads, width = query.shape
    vmem = pl.BlockSpec(memory_space=pltpu.VMEM)
    return pl.pallas_call(
        route_body,
        out_shape=(
            jax.ShapeDtypeStruct((slots, width), BF16),
            jax.ShapeDtypeStruct((reads, width), F32),
            jax.ShapeDtypeStruct((reads, LANES), F32),
        ),
        in_specs=[pl.BlockSpec(memory_space=pltpu.SMEM)] + [vmem] * 8,
        out_specs=(vmem,) * 3,
        scratch_shapes=[pltpu.VMEM((reads, width), F32)],
        name="route",
    )(ids, state, query, lifts, attended, resid, gain, router, score)


def slope_body(
    ids_ref, returned_ref, unit_ref, small_ref, gain_ref, router_ref, score_ref, slope_ref, told_ref,
):
    reads, width = unit_ref.shape
    slots = returned_ref.shape[0]
    experts = router_ref.shape[0]
    capacity = slots // experts
    where = targets(ids_ref, capacity)
    spots = [column([where[r][k] for r in range(reads)]) for k in range(2)]
    inverse, first, own = (small_ref[:, i : i + 1] for i in range(3))
    gates = (first, 1.0 - first)
    d_in = jnp.zeros((reads, width), F32)
    scores = [jnp.zeros((reads, 1), F32) for _ in range(2)]
    for slot in range(slots):
        row = returned_ref[slot : slot + 1, :width].astype(F32)
        told = returned_ref[slot : slot + 1, width : width + 1].astype(F32)
        weight = jnp.where(spots[0] == slot, gates[0], 0.0) + jnp.where(spots[1] == slot, gates[1], 0.0)
        d_in = d_in + weight * row
        scores = [s + jnp.where(spot == slot, told, 0.0) for s, spot in zip(scores, spots)]
    own = own + gates[0] * scores[0] + gates[1] * scores[1]
    d_logit = (scores[0] - scores[1]) * gates[0] * gates[1]
    columns = jnp.zeros((reads, width), F32)
    picks = [column([ids_ref[r, k] for r in range(reads)]) for k in range(2)]
    for name in range(experts):
        sign = (picks[0] == name).astype(F32) - (picks[1] == name).astype(F32)
        columns = columns + sign * router_ref[name : name + 1, :].astype(F32)
    d_unit = (d_in + d_logit * columns) * gain_ref[...].astype(F32)
    unit = unit_ref[...]
    mean = jnp.sum(d_unit * unit, axis=1, keepdims=True) * (1.0 / width)
    slope = score_ref[...].astype(F32) + inverse * (d_unit - unit * mean)
    slope_ref[...] = slope
    told_ref[...] = jnp.broadcast_to(jnp.sum(own, axis=0, keepdims=True), told_ref.shape)


def pack_body(told_ref, slope_ref, lifted_ref, total_ref, payload_ref):
    count = told_ref.shape[0]
    width = slope_ref.shape[1]
    heads = total_ref.shape[1]
    payload_ref[:, :width] = jnp.concatenate(
        [slope_ref[...], lifted_ref[...].astype(F32)], axis=0
    ).astype(BF16)
    total = jnp.concatenate(list(parts_of(total_ref[...])) + [jnp.zeros((1, heads), F32)], axis=0)
    total = jnp.concatenate([total, jnp.zeros((4, LANES - heads), F32)], axis=1)
    sub = lax.broadcasted_iota(jnp.int32, (count, LANES), 0)
    lane = lax.broadcasted_iota(jnp.int32, (count, LANES), 1)
    told = jnp.zeros((1, LANES), F32)
    for i, part in enumerate(parts_of(told_ref[...])):
        told = told + jnp.sum(jnp.where(lane == sub + i * count, part, 0.0), axis=0, keepdims=True)
    row = lax.broadcasted_iota(jnp.int32, (4, LANES), 0)
    meta = jnp.where(row == 3, told, total)
    payload_ref[:, width:] = jnp.concatenate([meta, jnp.zeros((4, LANES), F32)], axis=0).astype(BF16)


def pack(told, slope, lifted, total):
    reads, width = slope.shape
    vmem = pl.BlockSpec(memory_space=pltpu.VMEM)
    return pl.pallas_call(
        pack_body,
        out_shape=jax.ShapeDtypeStruct((2 * reads, width + LANES), BF16),
        in_specs=[vmem] * 4,
        out_specs=vmem,
        name="pack",
    )(told, slope, lifted, total)


def slope_of(ids, returned, unit, small, gain, router, score, copies):
    reads, width = unit.shape
    vmem = pl.BlockSpec(memory_space=pltpu.VMEM)
    return pl.pallas_call(
        slope_body,
        out_shape=(
            jax.ShapeDtypeStruct((reads, width), F32),
            jax.ShapeDtypeStruct((copies, LANES), F32),
        ),
        in_specs=[pl.BlockSpec(memory_space=pltpu.SMEM)] + [vmem] * 6,
        out_specs=(vmem,) * 2,
        name="slope",
    )(ids, returned, unit, small, gain, router, score)


def arrange_body(*refs):
    out_ref = refs[-1]
    half = refs[0].shape[0] // 2
    blocks = [ref[...].astype(F32) for ref in refs[:-1]]
    rows = [block[:half] for block in blocks] + [block[half:] for block in blocks]
    out_ref[...] = jnp.concatenate(rows, axis=0).astype(BF16)


def arrange(blocks):
    rows, width = blocks[0].shape
    vmem = pl.BlockSpec(memory_space=pltpu.VMEM)
    return pl.pallas_call(
        arrange_body,
        out_shape=jax.ShapeDtypeStruct((rows * len(blocks), width), BF16),
        in_specs=[vmem] * len(blocks),
        out_specs=vmem,
        name="arrange",
    )(*blocks)


def prefix_body(bound_ref, terms_ref, out_ref):
    blocks, rows, lanes = out_ref.shape
    near = lax.broadcasted_iota(jnp.int32, (rows, lanes), 0) < bound_ref[0]
    state = jnp.zeros((rows, lanes), jnp.float32)
    for block in range(blocks):
        out_ref[block] = state.astype(jnp.bfloat16)
        tail = terms_ref[block, rows : rows + 8, :].astype(jnp.float32)
        one = jnp.exp(tail[0:1] + tail[1:2] + tail[2:3])
        two = jnp.exp(tail[3:4] + tail[4:5] + tail[5:6])
        state = state * jnp.where(near, one, two) + terms_ref[block, :rows, :].astype(jnp.float32)

def exclusive_states(payload):
    count, rows, lanes = payload.shape
    rows = rows - 8
    size = lanes // 2
    place = lax.axis_index("seq")
    arrived = lax.all_to_all(payload, "seq", 0, 0, tiled=True)
    bound = ((place * rows) // size + 1) * size - place * rows
    vmem = pl.BlockSpec(memory_space=pltpu.VMEM)
    sums = pl.pallas_call(
        prefix_body,
        out_shape=jax.ShapeDtypeStruct((count, rows, lanes), BF16),
        in_specs=[pl.BlockSpec(memory_space=pltpu.SMEM), vmem],
        out_specs=vmem,
        name="state_prefix",
    )(bound.reshape(1), arrived)
    back = lax.all_to_all(sums, "seq", 0, 0, tiled=True)
    return back.reshape(count * rows // size, size, lanes)


def per_device(
    resid_rows,
    query_rows,
    key_rows,
    value_rows,
    log_decay,
    read_pos,
    expert_ids,
    pair_order,
    lengths,
    norm_gain,
    router_weight,
    score_weight,
    gate_weight,
    up_weight,
    down_weight,
):
    seq_count = lax.axis_size("seq")
    exp_count = lax.axis_size("exp")
    seq_index = lax.axis_index("seq")
    exp_index = lax.axis_index("exp")
    zs = seq_count // YS
    token_count = key_rows.shape[1]
    model_width = key_rows.shape[2]
    read_count = query_rows.shape[1]
    expert_count = router_weight.shape[1]
    capacity = max(2, 4 * read_count // exp_count)
    slot_count = expert_count * capacity
    wide = model_width + LANES
    keys, values, query = key_rows[0], value_rows[0], query_rows[0]
    ids = expert_ids[0].astype(jnp.int32)
    gain = norm_gain.reshape(1, model_width)
    score = score_weight.reshape(1, model_width)
    router = router_weight.T
    place = jnp.stack([seq_index, jnp.int32(YS), exp_index]).astype(jnp.int32)

    payload, lifted, total, tails, lifts, weights, scores, attended = prepare(
        read_pos[0] - seq_index * token_count, keys, values, query, log_decay[0], seq_count
    )
    state = exclusive_states(payload)
    outgoing, unit, small = route(
        ids, state, query, lifts, attended, resid_rows[0], gain, router, score, slot_count
    )
    arrived = lax.all_to_all(
        outgoing.reshape(expert_count, capacity, model_width), "exp", 0, 0, tiled=True
    ).reshape(slot_count, model_width)
    piece = gather_slots(arrived).reshape(seq_count * slot_count, model_width)

    gate_w = gate_weight[0]
    up_w = up_weight[0]
    down_w = down_weight[0]
    down_score = jnp.sum(down_w.astype(F32) * score.astype(F32), axis=1)
    pre_gate = jnp.dot(piece, gate_w, preferred_element_type=F32)
    pre_up = jnp.dot(piece, up_w, preferred_element_type=F32)
    gate_sigmoid = jax.nn.sigmoid(pre_gate)
    silu = pre_gate * gate_sigmoid
    slot_score = jnp.sum(silu * pre_up * down_score[None, :], axis=1)
    d_pre_gate = (
        down_score[None, :] * pre_up * gate_sigmoid * (1.0 + pre_gate * (1.0 - gate_sigmoid))
    ).astype(BF16)
    d_pre_up = (down_score[None, :] * silu).astype(BF16)
    back = jnp.einsum("sf,df->sd", d_pre_gate, gate_w, preferred_element_type=F32)
    back = back + jnp.einsum("sf,df->sd", d_pre_up, up_w, preferred_element_type=F32)
    score_cols = jnp.pad(slot_score[:, None], ((0, 0), (0, LANES - 1)))
    terms = jnp.concatenate([back, score_cols], axis=1).astype(BF16)
    summed = reduce_slots(terms.reshape(zs, YS, slot_count, wide))
    returned = lax.all_to_all(
        summed.reshape(expert_count, capacity, wide), "exp", 0, 0, tiled=True
    ).reshape(slot_count, wide)

    slope, told = slope_of(ids, returned, unit, small, gain, router, score, exp_count)
    told = lax.all_to_all(told.reshape(exp_count, 1, LANES), "exp", 0, 0, tiled=True)
    rows = pack(told.reshape(exp_count, LANES), slope, lifted, total)
    rows = arrange(direct_gather(rows, "y", YS))
    rows = jnp.stack(ring_gather(rows, "z", zs, False))
    meta = rows[:, : YS * read_count, model_width:].reshape(seq_count, read_count, LANES)
    parts = meta.transpose(1, 0, 2)
    loss, grad_query, grad_resid, grad_keys, grad_values = finish(
        place,
        pair_order,
        lengths,
        keys,
        values,
        query,
        slope,
        rows,
        parts,
        state,
        tails,
        lifts,
        weights,
        scores,
        span=token_count * seq_count,
        length_weight=LENGTH_WEIGHT,
        score_scale=SCORE_SCALE,
    )
    return (loss.reshape(()), grad_query[None], grad_resid[None], grad_keys[None], grad_values[None])


def solution(mesh):
    in_specs = (
        P("exp", "seq", None),
        P("exp", "seq", None),
        P("exp", "seq", None),
        P("exp", "seq", None),
        P("exp", None, "seq"),
        P("exp", "seq"),
        P("exp", "seq", None),
        P(),
        P(),
        P(),
        P(),
        P(),
        P("exp", None, "seq"),
        P("exp", None, "seq"),
        P("exp", "seq", None),
    )
    out_specs = (
        P(),
        P("exp", "seq", None),
        P("exp", "seq", None),
        P("exp", "seq", None),
        P("exp", "seq", None),
    )
    return jax.shard_map(
        per_device, mesh=mesh, in_specs=in_specs, out_specs=out_specs, check_vma=False
    )
```
